768 devices in a mesh: dp: 32 (over y, x), head: 24 (over z, core).
Axes of the slice: x: 4, y: 8, z: 12, core: 2. Of those that a mesh axis runs over, the one named last changes fastest.
Arguments:
- queries: bfloat16 [12288, 3072], P('dp', 'head'), may hold values from -8 to 8
- keys: bfloat16 [12288, 384], P('dp'), may hold values from -5 to 5
- values: bfloat16 [12288, 384], P('dp'), may hold values from -6 to 6
- block_of_slot: int32 [64], replicated, may hold values from 0 to 63, as said below
- doc_lengths: int32 [4], replicated, may hold values from 1 to 6144, 12288 in all
- out_weight: bfloat16 [3072, 2048], P('head'), may hold values from -0.5 to 0.5
Outputs:
- mixed: bfloat16 [12288, 2048], P(('dp', 'head'))
The draws below stay inside these ranges and needn't reach their ends.
Inputs may be any that keep to these rules, and one draw needn't show every extreme that they name: `block_of_slot`: a permutation of 0 .. 63; entries 2 i and 2 i + 1 are the two slots of index i of dp, and they add to 63.
All inputs are finite; a program needn't handle non-finite values.
Results may differ from the reference program's by a relative error of at most 0.02.
Values may be sent and summed in bfloat16 or wider, within the bound.
No kernel may reach another device: no remote copies, remote signals or barrier semaphores. Data moves between devices by JAX's collectives and lax.ppermute only.
A program may use at most 32 MiB of HBM per device.

```python
import math
import jax
import jax.numpy as jnp
import numpy as np
from jax import lax

D = 2048
HD = 128
QHEADS = 24
GROUP = 8
KVH = 3
TOK_DEV = 384
HALF = 192
TOKENS = 12288
BLOCKS = 64
DOCS = 4


def shared_draw(key):
    base = jax.random.fold_in(key, 7)
    key_vals = jnp.clip(jax.random.normal(jax.random.fold_in(base, 5), (TOKENS, KVH, HD), jnp.float32), -4.0, 4.0)
    query_vals = 1.5 * jnp.clip(jax.random.normal(jax.random.fold_in(base, 6), (TOKENS, QHEADS, HD), jnp.float32), -4.0, 4.0)
    return (query_vals.reshape(TOKENS, QHEADS * HD), key_vals.reshape(TOKENS, KVH * HD))


def draw_queries(key, part):
    return shared_draw(key)[0].astype(jnp.bfloat16)


def draw_keys(key, part):
    return shared_draw(key)[1].astype(jnp.bfloat16)


def draw_block_of_slot(key, part):
    order = jax.random.permutation(jax.random.fold_in(key, 11), BLOCKS // 2)
    table = jnp.stack([order, BLOCKS - 1 - order], axis=1).reshape(BLOCKS)
    return table.astype(jnp.int32)


def block_scale(stream_key, extent, pieces, least, top_value):
    gain, own = 1.0, jax.random.fold_in(stream_key, 6)
    for position, parts in pieces:
        heights = jnp.exp(jax.random.uniform(jax.random.fold_in(own, position), (parts,), jnp.float32, least / len(pieces), top_value / len(pieces)))
        gain = gain * jnp.repeat(heights, extent[position] // parts).reshape([-1 if axis == position else 1 for axis in range(len(extent))])
    return gain


def split_up(amount, total, reach, slope):
    weights = [(1 << 20) // math.isqrt(standing ** slope) + 1 for standing in range(2, amount + 1)]
    surplus, given = total - reach - (amount - 1), [1] * (amount - 1)
    while surplus > 0:
        movable = [i for i in range(amount - 1) if given[i] < reach]
        mass, budget = sum([weights[i] for i in movable]), surplus
        for i in movable:
            extra = min(reach - given[i], max(1, budget * weights[i] // mass), surplus)
            given[i] = given[i] + extra
            surplus = surplus - extra
    return np.array([reach] + given)


def ragged_sizes(own_key, count, total, most, slope):
    if count == 2:
        one = jax.random.randint(own_key, (), max(1, total - most), min(most, total - 1) + 1)
        return jnp.stack([one, total - one])
    lengths = jnp.asarray(split_up(count, total, most, slope), jnp.int32)
    couples = (count - 1) // 2
    giver, sink = lengths[1:1 + 2 * couples:2], lengths[2:2 + 2 * couples:2]
    margin = jnp.minimum(giver - 1, most - sink)
    shifted = jax.random.randint(jax.random.fold_in(own_key, 1), (couples,), 0, 1 << 20) % (margin + 1)
    lengths = lengths.at[1:1 + 2 * couples:2].set(giver - shifted).at[2:2 + 2 * couples:2].set(sink + shifted)
    return lengths[jax.random.permutation(jax.random.fold_in(own_key, 2), count)]


def noise(key, shape, scale, most, cuts=(), kind=jnp.bfloat16):
    entries = scale * jax.random.normal(key, shape, jnp.float32)
    if cuts:
        entries = entries * block_scale(key, shape, cuts, -0.22, 0.18)
    return jnp.clip(entries, -most, most).astype(kind)


def setup_inputs(seed: int = 0) -> dict:
    key_of = jax.random.split(jax.random.key(seed), 7)
    return {
        "queries": draw_queries(jax.random.fold_in(key_of[6], 71), 0),
        "keys": draw_keys(jax.random.fold_in(key_of[6], 71), 0),
        "values": noise(key_of[2], (TOKENS, KVH * HD), 1.0, 6.0, ((0, 32),)),
        "block_of_slot": draw_block_of_slot(jax.random.fold_in(key_of[6], 71), 0),
        "doc_lengths": ragged_sizes(key_of[4], DOCS, TOKENS, TOKENS // 2, 2).astype(jnp.int32),
        "out_weight": noise(key_of[5], (QHEADS * HD, D), HD ** -0.5, 0.5, ((0, 24),)),
    }


def reference(queries, keys, values, block_of_slot, doc_lengths, out_weight):
    row_index = jnp.arange(TOKENS, dtype=jnp.int32)
    positions = block_of_slot[row_index // HALF] * HALF + row_index % HALF
    bounds = jnp.cumsum(doc_lengths)[:-1]
    documents = lax.optimization_barrier(jnp.sum((positions[:, None] >= bounds[None, :]).astype(jnp.int32), axis=1))
    score_scale = 1.0 / math.sqrt(HD)
    block_count = TOKENS // TOK_DEV
    query_blocks = queries.reshape(block_count, TOK_DEV, QHEADS * HD)
    pos_blocks = positions.reshape(block_count, TOK_DEV)
    doc_blocks = documents.reshape(block_count, TOK_DEV)

    def one_head(head_index):
        kv_start = head_index // GROUP * HD
        head_keys = lax.dynamic_slice_in_dim(keys, kv_start, HD, 1)
        head_values = lax.dynamic_slice_in_dim(values, kv_start, HD, 1)

        def one_block(inputs):
            query_rows, query_pos, query_doc = inputs
            head_queries = lax.dynamic_slice_in_dim(query_rows, head_index * HD, HD, 1)
            scores = jnp.dot(head_queries, head_keys.T, preferred_element_type=jnp.float32) * score_scale
            allowed = (query_doc[:, None] == documents[None, :]) & (positions[None, :] <= query_pos[:, None])
            masked = jnp.where(allowed, scores, -jnp.inf)
            row_max = lax.optimization_barrier(jnp.max(masked, axis=1, keepdims=True))
            weights = jnp.where(allowed, jnp.exp(masked - row_max), 0.0)
            numerator = jnp.dot(weights.astype(jnp.bfloat16), head_values, preferred_element_type=jnp.float32)
            return (numerator / lax.optimization_barrier(jnp.sum(weights, axis=1, keepdims=True))).astype(jnp.bfloat16)
        return lax.map(one_block, (query_blocks, pos_blocks, doc_blocks))
    attended = lax.map(one_head, jnp.arange(QHEADS, dtype=jnp.int32))
    attended = attended.transpose(1, 2, 0, 3).reshape(TOKENS, QHEADS * HD)

    def add_head(total, head_index):
        head_cols = lax.dynamic_slice_in_dim(attended, head_index * HD, HD, 1)
        head_rows = lax.dynamic_slice_in_dim(out_weight, head_index * HD, HD, 0)
        term = jnp.dot(head_cols, head_rows, preferred_element_type=jnp.float32)
        rounded = lax.optimization_barrier(term.astype(jnp.bfloat16))
        return (total + rounded.astype(jnp.float32), None)
    total, _ = lax.scan(add_head, jnp.zeros((TOKENS, D), jnp.float32), jnp.arange(QHEADS, dtype=jnp.int32))
    return total.astype(jnp.bfloat16)
```

```python
import math

import jax
import jax.numpy as jnp
from jax import lax
from jax.experimental import pallas as pl
from jax.experimental.pallas import tpu as pltpu
from jax.sharding import Mesh, PartitionSpec as P

AXES = ("y", "xh", "xl", "zh", "zm", "zl", "core")
SIZES = (8, 2, 2, 3, 2, 2, 2)
DP = ("y", "xh", "xl")
HEAD = ("zh", "zm", "zl", "core")
KV_AXES = ("y", "xh")
TEAM = ("xl", "zl", "core")
Z6 = ("zh", "zm")

TOK = 384
HALF = 192
HD = 128
QUART = 48
SRC = 16
PIECES = 2 * SRC
CHUNK = 256
KEYS = PIECES * QUART
PAD = KEYS + CHUNK
TILE = 4 * HALF
TEAM_SIZE = 8
STAT = 16
SEND = TOK + STAT
LOW = -1e30
FAR = 1 << 20
SCALE = math.log2(math.e) / math.sqrt(HD)


def spread_kernel(at_ref, k_hbm, v_hbm, out_hbm, buf, in_sem, out_sem):
    row = pl.multiple_of(at_ref[0] * QUART, 16)
    col = pl.multiple_of(at_ref[1] * HD, HD)
    loads = []
    for n, src in enumerate((k_hbm, v_hbm)):
        for half in range(2):
            loads.append(
                pltpu.make_async_copy(
                    src.at[pl.ds(half * HALF + row, QUART), pl.ds(col, HD)],
                    buf.at[pl.ds((2 * n + half) * QUART, QUART), :],
                    in_sem.at[2 * n + half],
                )
            )
    for copy in loads:
        copy.start()
    for copy in loads:
        copy.wait()
    stores = [
        pltpu.make_async_copy(buf, out_hbm.at[n], out_sem.at[n]) for n in range(SRC)
    ]
    for copy in stores:
        copy.start()
    for copy in stores:
        copy.wait()


def attend_kernel(
    rank_ref,
    sorted_ref,
    tile_ref,
    kv_ref,
    q_ref,
    kpos_ref,
    qpos_ref,
    qstart_ref,
    out_ref,
    k_scr,
    v_scr,
    q_scr,
    s_scr,
    m_scr,
    l_scr,
    acc_scr,
    st_scr,
):
    for piece in range(PIECES):
        src, half = divmod(piece, 2)
        at = pl.multiple_of(rank_ref[piece] * QUART, 16)
        k_scr[pl.ds(at, QUART), :] = kv_ref[src, half * QUART : (half + 1) * QUART, :]
        v_scr[pl.ds(at, QUART), :] = kv_ref[
            src, (2 + half) * QUART : (3 + half) * QUART, :
        ]
    k_scr[KEYS:, :] = jnp.zeros((CHUNK, HD), jnp.bfloat16)
    v_scr[KEYS:, :] = jnp.zeros((CHUNK, HD), jnp.bfloat16)
    st_scr[...] = jnp.zeros_like(st_scr)
    for tile in range(4):
        xl, half = divmod(tile, 2)
        for d in range(4):
            for j in range(4):
                for z3 in range(3):
                    to = d * HALF + j * QUART + z3 * 16
                    of = half * HALF + z3 * 64 + d * 16
                    q_scr[tile, to : to + 16, :] = q_ref[xl * 4 + j, of : of + 16, :]

    def one_tile(tile, carry):
        low, steps, q_first, start_last = (tile_ref[tile, n] for n in range(4))
        m_scr[...] = jnp.full_like(m_scr, LOW)
        l_scr[...] = jnp.zeros_like(l_scr)
        acc_scr[...] = jnp.zeros_like(acc_scr)

        def one_step(step, carry):
            first = low * QUART + step * CHUNK
            at = pl.multiple_of(first, 16)
            s_scr[...] = lax.dot_general(
                k_scr[pl.ds(at, CHUNK), :],
                q_scr[tile],
                (((1,), (1,)), ((), ())),
                preferred_element_type=jnp.float32,
            )
            first_pos = sorted_ref[first // QUART] * HALF
            last_pos = sorted_ref[(first + CHUNK - 1) // QUART] * HALF + HALF - 1

            @pl.when((last_pos > q_first) | (first_pos < start_last))
            def _():
                key_pos = kpos_ref[pl.ds(at, CHUNK), :]
                allowed = (key_pos <= qpos_ref[pl.ds(tile, 1), :]) & (
                    key_pos >= qstart_ref[pl.ds(tile, 1), :]
                )
                s_scr[...] = jnp.where(allowed, s_scr[...], LOW)

            scores = s_scr[...]
            old = m_scr[...]
            new = jnp.maximum(old, jnp.max(scores, axis=0, keepdims=True))
            m_scr[...] = new
            probs = jnp.exp2((scores - new) * SCALE)
            factor = jnp.exp2((old - new) * SCALE)
            l_scr[...] = l_scr[...] * factor + jnp.sum(probs, axis=0, keepdims=True)
            acc_scr[...] = acc_scr[...] * factor + lax.dot_general(
                v_scr[pl.ds(at, CHUNK), :],
                probs.astype(jnp.bfloat16),
                (((0,), (0,)), ((), ())),
                preferred_element_type=jnp.float32,
            )
            return carry

        lax.fori_loop(0, steps, one_step, 0)
        total = jnp.where(l_scr[...] > 0, l_scr[...], 1.0)
        part = (acc_scr[...] / total).T.astype(jnp.bfloat16)
        lse = m_scr[...] * SCALE + jnp.log2(total)
        high = lse.astype(jnp.bfloat16).astype(jnp.float32)
        mid = (lse - high).astype(jnp.bfloat16).astype(jnp.float32)
        stats = (high, mid, lse - high - mid)
        xl4 = (tile // 2) * 4
        half = tile % 2
        rows = pl.multiple_of(half * HALF, 16)
        for d in range(4):
            out_ref[xl4 + d, pl.ds(rows, HALF), :] = part[d * HALF : (d + 1) * HALF]
            for n, stat in enumerate(stats):
                if d % 2:
                    stat = pltpu.roll(
                        jnp.broadcast_to(stat, (8, TILE)), TILE - 64, 1
                    )[:1]
                base = d * HALF - (d % 2) * 64
                for w in range(2):
                    st_scr[xl4 + d, pl.ds(half * 6 + n * 2 + w, 1), :] = stat[
                        :, base + w * 128 : base + (w + 1) * 128
                    ]
        return carry

    lax.fori_loop(0, 4, one_tile, 0)
    for dest in range(TEAM_SIZE):
        out_ref[dest, TOK:, :] = st_scr[dest].astype(jnp.bfloat16)


def project_kernel(at_ref, got_ref, w0_ref, w1_ref, out_ref, att_scr):
    for half in range(2):
        sides = []
        for w in range(2):
            lse = []
            for k in range(TEAM_SIZE):
                stat = got_ref[k, TOK:, :].astype(jnp.float32)
                row = half * 6 + w
                lse.append(
                    stat[row : row + 1] + stat[row + 2 : row + 3] + stat[row + 4 : row + 5]
                )
            lse = jnp.concatenate(lse, axis=0)
            weight = jnp.exp2(lse - jnp.max(lse, axis=0, keepdims=True))
            weight = weight / jnp.sum(weight, axis=0, keepdims=True)
            sides.append(weight.T)
        weight = jnp.concatenate([sides[0], sides[1][:64]], axis=0)
        total = jnp.zeros((HALF, HD), jnp.float32)
        for k in range(TEAM_SIZE):
            total += weight[:, k : k + 1] * got_ref[
                k, half * HALF : (half + 1) * HALF, :
            ].astype(jnp.float32)
        att_scr[half] = total.astype(jnp.bfloat16)
    own = at_ref[0]
    out = None
    for n, (w_ref, part, flip) in enumerate(
        ((w0_ref, 0, 0), (w0_ref, 1, 2), (w1_ref, 0, 1), (w1_ref, 1, 3))
    ):
        rows = pl.multiple_of((own ^ flip) * QUART, 16)
        att = jnp.concatenate(
            [att_scr[half, pl.ds(rows, QUART), :] for half in range(2)], axis=0
        )
        term = jnp.dot(att, w_ref[part], preferred_element_type=jnp.float32)
        out = term if out is None else out + term
    out_ref[...] = out.astype(jnp.bfloat16)


def doc_start(pos, bounds):
    start = jnp.zeros_like(pos)
    for n in range(bounds.shape[0]):
        start = jnp.where(pos >= bounds[n], jnp.maximum(start, bounds[n]), start)
    return start


def per_device(queries, keys, values, block_of_slot, doc_lengths, out_weight):
    zl, core = lax.axis_index("zl"), lax.axis_index("core")
    own = zl * 2 + core
    at = jnp.stack([own, lax.axis_index("zh")]).astype(jnp.int32)
    any_spec = pl.BlockSpec(memory_space=pl.ANY)
    smem = pl.BlockSpec(memory_space=pltpu.SMEM)
    vmem = pl.BlockSpec(memory_space=pltpu.VMEM)
    spread = pl.pallas_call(
        spread_kernel,
        out_shape=jax.ShapeDtypeStruct((SRC, 4 * QUART, HD), jnp.bfloat16),
        in_specs=[smem, any_spec, any_spec],
        out_specs=any_spec,
        scratch_shapes=[
            pltpu.VMEM((4 * QUART, HD), jnp.bfloat16),
            pltpu.SemaphoreType.DMA((4,)),
            pltpu.SemaphoreType.DMA((SRC,)),
        ],
        name="spread",
    )(at, keys, values)
    kv = lax.all_to_all(spread, KV_AXES, 0, 0, tiled=True)
    q = lax.all_gather(queries, TEAM, axis=0)
    flip = [(0, 1), (1, 0)]
    w_side = lax.ppermute(out_weight, "zl", flip)
    w0 = jnp.stack([out_weight, w_side])
    w1 = lax.ppermute(w0, "core", flip)

    table = block_of_slot.reshape(8, 2, 2, 2)
    xl = lax.axis_index("xl")
    blocks = jnp.where(xl == 0, table[:, :, 0], table[:, :, 1]).reshape(PIECES)
    rank = jnp.sum((blocks[None, :] < blocks[:, None]).astype(jnp.int32), axis=1)
    slots = jnp.arange(PIECES, dtype=jnp.int32)
    in_order = jnp.sum(
        jnp.where(rank[None, :] == slots[:, None], blocks[None, :], 0), axis=1
    )
    bounds = jnp.cumsum(doc_lengths)[:-1]
    key_pos = (
        in_order[:, None] * HALF + own * QUART + jnp.arange(QUART, dtype=jnp.int32)
    ).reshape(KEYS, 1)
    key_pos = jnp.concatenate([key_pos, jnp.full((PAD - KEYS, 1), FAR, jnp.int32)])
    in_order_pad = jnp.concatenate(
        [in_order, jnp.full(((PAD - KEYS) // QUART + 1,), FAR // HALF, jnp.int32)]
    )
    here = lax.axis_index("y") * 2 + lax.axis_index("xh")
    q_block = jnp.sum(
        jnp.where(
            jnp.arange(SRC, dtype=jnp.int32)[:, None] == here,
            block_of_slot.reshape(SRC, 4),
            0,
        ),
        axis=0,
    )
    lane = jnp.arange(TILE, dtype=jnp.int32)
    in_half = (lane % QUART) // 16 * 64 + lane // HALF * 16 + lane % 16
    q_pos = q_block[:, None] * HALF + in_half[None, :]
    q_start = doc_start(q_pos, bounds)
    first_start = doc_start(q_block * HALF, bounds)
    last_start = doc_start(q_block * HALF + HALF - 1, bounds)
    low = jnp.sum(
        (blocks[None, :] < first_start[:, None] // HALF).astype(jnp.int32), axis=1
    )
    high = jnp.sum((blocks[None, :] <= q_block[:, None]).astype(jnp.int32), axis=1)
    steps = ((high - low) * QUART + CHUNK - 1) // CHUNK
    tiles = jnp.stack([low, steps, q_block * HALF, last_start], axis=1)

    sent = pl.pallas_call(
        attend_kernel,
        out_shape=jax.ShapeDtypeStruct((TEAM_SIZE, SEND, HD), jnp.bfloat16),
        in_specs=[smem, smem, smem, vmem, vmem, vmem, vmem, vmem],
        out_specs=vmem,
        scratch_shapes=[
            pltpu.VMEM((PAD, HD), jnp.bfloat16),
            pltpu.VMEM((PAD, HD), jnp.bfloat16),
            pltpu.VMEM((4, TILE, HD), jnp.bfloat16),
            pltpu.VMEM((CHUNK, TILE), jnp.float32),
            pltpu.VMEM((1, TILE), jnp.float32),
            pltpu.VMEM((1, TILE), jnp.float32),
            pltpu.VMEM((HD, TILE), jnp.float32),
            pltpu.VMEM((TEAM_SIZE, STAT, HD), jnp.float32),
        ],
        compiler_params=pltpu.CompilerParams(vmem_limit_bytes=32 << 20),
        cost_estimate=pl.CostEstimate(
            flops=4 * 4 * TILE * KEYS * HD,
            transcendentals=4 * TILE * KEYS,
            bytes_accessed=4 << 20,
        ),
        name="attend",
    )(rank, in_order_pad, tiles, kv, q, key_pos, q_pos, q_start)
    got = lax.all_to_all(sent, TEAM, 0, 0, tiled=True)
    terms = pl.pallas_call(
        project_kernel,
        out_shape=jax.ShapeDtypeStruct((TOK // 4, out_weight.shape[1]), jnp.bfloat16),
        in_specs=[smem, vmem, vmem, vmem],
        out_specs=vmem,
        scratch_shapes=[pltpu.VMEM((2, HALF, HD), jnp.bfloat16)],
        compiler_params=pltpu.CompilerParams(vmem_limit_bytes=32 << 20),
        name="project",
    )(at, got, w0, w1)
    parts = lax.all_to_all(terms.reshape(6, 16, -1), Z6, 0, 0, tiled=True)
    return jnp.sum(parts.astype(jnp.float32), axis=0).astype(jnp.bfloat16)


def solution(mesh):
    fine = Mesh(mesh.devices.reshape(SIZES), AXES)
    return jax.shard_map(
        per_device,
        mesh=fine,
        in_specs=(P(DP, HEAD), P(DP, None), P(DP, None), P(), P(), P(HEAD, None)),
        out_specs=P(DP + HEAD, None),
        check_vma=False,
    )
```

```python
import math

import jax
import jax.numpy as jnp
import numpy as np
from jax import lax
from jax.experimental import pallas as pl
from jax.experimental.pallas import tpu as pltpu
from jax.sharding import Mesh, PartitionSpec as P

AXES = ("y", "xh", "xl", "zh", "zm", "zl", "core")
SIZES = (8, 2, 2, 3, 2, 2, 2)
DP = ("y", "xh", "xl")
HEAD = ("zh", "zm", "zl", "core")
KV_AXES = ("y", "xh")
TEAM = ("xl", "zl", "core")
Z6 = ("zh", "zm")

TOK = 384
HALF = 192
HD = 128
QUART = 48
SRC = 16
PIECES = 2 * SRC
CHUNK = 256
KEYS = PIECES * QUART
PAD = KEYS + CHUNK
SLOTS = PIECES + CHUNK // QUART + 2
TILE = 4 * HALF
TEAM_SIZE = 8
STAT = 16
SEND = TOK + STAT
LOW = -1e30
FAR = 1 << 20
SCALE = math.log2(math.e) / math.sqrt(HD)


def spread_kernel(k_hbm, v_hbm, out_hbm, buf, in_sem, out_sem):
    own = lax.axis_index("zl") * 2 + lax.axis_index("core")
    row = pl.multiple_of(own * QUART, 16)
    col = pl.multiple_of(lax.axis_index("zh") * HD, HD)
    loads = []
    for n, src in enumerate((k_hbm, v_hbm)):
        for half in range(2):
            loads.append(
                pltpu.make_async_copy(
                    src.at[pl.ds(half * HALF + row, QUART), pl.ds(col, HD)],
                    buf.at[pl.ds((2 * n + half) * QUART, QUART), :],
                    in_sem.at[2 * n + half],
                )
            )
    for copy in loads:
        copy.start()
    for copy in loads:
        copy.wait()
    stores = [
        pltpu.make_async_copy(buf, out_hbm.at[n], out_sem.at[n]) for n in range(SRC)
    ]
    for copy in stores:
        copy.start()
    for copy in stores:
        copy.wait()


def start_of(pos, bounds):
    start = jnp.zeros_like(pos)
    for bound in bounds:
        start = jnp.where(pos >= bound, jnp.maximum(start, bound), start)
    return start


def table_kernel(
    slot_ref,
    len_ref,
    lane_ref,
    q_ref,
    rank_ref,
    sorted_ref,
    tile_ref,
    qpos_ref,
    qstart_ref,
    tiles_ref,
    where_scr,
    before_scr,
):
    xl = lax.axis_index("xl")
    here = lax.axis_index("y") * 2 + lax.axis_index("xh")

    def clear(n, carry):
        where_scr[n] = PIECES
        return carry

    lax.fori_loop(0, 2 * PIECES, clear, 0)
    for piece in range(PIECES):
        src, half = divmod(piece, 2)
        where_scr[slot_ref[4 * src + 2 * xl + half]] = piece

    def walk(block, count):
        before_scr[block] = count
        piece = where_scr[block]
        rank_ref[piece] = count
        sorted_ref[count] = block
        return count + (piece < PIECES).astype(jnp.int32)

    before_scr[2 * PIECES] = lax.fori_loop(0, 2 * PIECES, walk, jnp.int32(0))
    for n in range(PIECES, SLOTS):
        sorted_ref[n] = FAR // HALF
    bounds = [len_ref[0]]
    for n in range(1, len_ref.shape[0] - 1):
        bounds.append(bounds[-1] + len_ref[n])
    lane = lane_ref[...]
    for tile in range(4):
        rel, half = divmod(tile, 2)
        block = slot_ref[4 * here + 2 * (xl ^ rel) + half]
        base = block * HALF
        low = before_scr[lax.div(start_of(base, bounds), HALF)]
        high = before_scr[block + 1]
        tile_ref[tile, 0] = low
        tile_ref[tile, 1] = lax.div((high - low) * QUART + CHUNK - 1, CHUNK)
        tile_ref[tile, 2] = base
        tile_ref[tile, 3] = start_of(base + HALF - 1, bounds)
        pos = lane + base
        qpos_ref[tile : tile + 1, :] = pos
        qstart_ref[tile : tile + 1, :] = start_of(pos, bounds)
        for d in range(4):
            for j in range(4):
                for z3 in range(3):
                    to = d * HALF + j * QUART + z3 * 16
                    of = half * HALF + z3 * 64 + d * 16
                    tiles_ref[tile, to : to + 16, :] = q_ref[j, rel, of : of + 16, :]


def attend_kernel(
    rank_ref,
    sorted_ref,
    tile_ref,
    kv_ref,
    q_ref,
    qpos_ref,
    qstart_ref,
    out_ref,
    kpos_scr,
    k_scr,
    v_scr,
    s_scr,
    m_scr,
    l_scr,
    acc_scr,
    st_scr,
):
    for piece in range(PIECES):
        src, half = divmod(piece, 2)
        at = pl.multiple_of(rank_ref[piece] * QUART, 16)
        k_scr[pl.ds(at, QUART), :] = kv_ref[src, half * QUART : (half + 1) * QUART, :]
        v_scr[pl.ds(at, QUART), :] = kv_ref[
            src, (2 + half) * QUART : (3 + half) * QUART, :
        ]
    k_scr[KEYS:, :] = jnp.zeros((CHUNK, HD), jnp.bfloat16)
    v_scr[KEYS:, :] = jnp.zeros((CHUNK, HD), jnp.bfloat16)
    st_scr[...] = jnp.zeros_like(st_scr)
    own = lax.axis_index("zl") * 2 + lax.axis_index("core")
    row = lax.broadcasted_iota(jnp.int32, (QUART, HD), 0) + own * QUART
    for n in range(PIECES):
        kpos_scr[n * QUART : (n + 1) * QUART, :] = row + sorted_ref[n] * HALF
    kpos_scr[KEYS:, :] = jnp.full((PAD - KEYS, HD), FAR, jnp.int32)

    def one_tile(tile, carry):
        low, steps, q_first, start_last = (tile_ref[tile, n] for n in range(4))
        m_scr[...] = jnp.full_like(m_scr, LOW)
        l_scr[...] = jnp.zeros_like(l_scr)
        acc_scr[...] = jnp.zeros_like(acc_scr)

        def one_step(step, carry):
            first = low * QUART + step * CHUNK
            at = pl.multiple_of(first, 16)
            s_scr[...] = lax.dot_general(
                k_scr[pl.ds(at, CHUNK), :],
                q_ref[tile],
                (((1,), (1,)), ((), ())),
                preferred_element_type=jnp.float32,
            )
            first_pos = sorted_ref[lax.div(first, QUART)] * HALF
            last_pos = sorted_ref[lax.div(first + CHUNK - 1, QUART)] * HALF + HALF - 1

            @pl.when((last_pos > q_first) | (first_pos < start_last))
            def _():
                key_pos = kpos_scr[pl.ds(at, CHUNK), :]
                key_pos = jnp.concatenate([key_pos] * (TILE // HD), axis=1)
                allowed = (key_pos <= qpos_ref[pl.ds(tile, 1), :]) & (
                    key_pos >= qstart_ref[pl.ds(tile, 1), :]
                )
                s_scr[...] = jnp.where(allowed, s_scr[...], LOW)

            scores = s_scr[...]
            old = m_scr[...]
            new = jnp.maximum(old, jnp.max(scores, axis=0, keepdims=True))
            m_scr[...] = new
            probs = jnp.exp2((scores - new) * SCALE)
            factor = jnp.exp2((old - new) * SCALE)
            l_scr[...] = l_scr[...] * factor + jnp.sum(probs, axis=0, keepdims=True)
            acc_scr[...] = acc_scr[...] * factor + lax.dot_general(
                v_scr[pl.ds(at, CHUNK), :],
                probs.astype(jnp.bfloat16),
                (((0,), (0,)), ((), ())),
                preferred_element_type=jnp.float32,
            )
            return carry

        lax.fori_loop(0, steps, one_step, 0)
        total = jnp.where(l_scr[...] > 0, l_scr[...], 1.0)
        part = (acc_scr[...] / total).T.astype(jnp.bfloat16)
        lse = m_scr[...] * SCALE + jnp.log2(total)
        high = lse.astype(jnp.bfloat16).astype(jnp.float32)
        mid = (lse - high).astype(jnp.bfloat16).astype(jnp.float32)
        stats = (high, mid, lse - high - mid)
        xl4 = ((tile >> 1) ^ lax.axis_index("xl")) * 4
        half = tile & 1
        rows = pl.multiple_of(half * HALF, 16)
        for d in range(4):
            out_ref[xl4 + d, pl.ds(rows, HALF), :] = part[d * HALF : (d + 1) * HALF]
            for n, stat in enumerate(stats):
                if d % 2:
                    stat = pltpu.roll(
                        jnp.broadcast_to(stat, (8, TILE)), TILE - 64, 1
                    )[:1]
                base = d * HALF - (d % 2) * 64
                for w in range(2):
                    st_scr[xl4 + d, pl.ds(half * 6 + n * 2 + w, 1), :] = stat[
                        :, base + w * 128 : base + (w + 1) * 128
                    ]
        return carry

    lax.fori_loop(0, 4, one_tile, 0)
    for dest in range(TEAM_SIZE):
        out_ref[dest, TOK:, :] = st_scr[dest].astype(jnp.bfloat16)


def project_kernel(got_ref, w0_ref, w1_ref, out_ref, att_scr):
    for half in range(2):
        sides = []
        for w in range(2):
            lse = []
            for k in range(TEAM_SIZE):
                stat = got_ref[k, TOK:, :].astype(jnp.float32)
                row = half * 6 + w
                lse.append(
                    stat[row : row + 1] + stat[row + 2 : row + 3] + stat[row + 4 : row + 5]
                )
            lse = jnp.concatenate(lse, axis=0)
            weight = jnp.exp2(lse - jnp.max(lse, axis=0, keepdims=True))
            weight = weight / jnp.sum(weight, axis=0, keepdims=True)
            sides.append(weight.T)
        weight = jnp.concatenate([sides[0], sides[1][:64]], axis=0)
        total = jnp.zeros((HALF, HD), jnp.float32)
        for k in range(TEAM_SIZE):
            total += weight[:, k : k + 1] * got_ref[
                k, half * HALF : (half + 1) * HALF, :
            ].astype(jnp.float32)
        att_scr[half] = total.astype(jnp.bfloat16)
    own = lax.axis_index("zl") * 2 + lax.axis_index("core")
    out = None
    for w_ref, part, flip in ((w0_ref, 0, 0), (w0_ref, 1, 2), (w1_ref, 0, 1), (w1_ref, 1, 3)):
        rows = pl.multiple_of((own ^ flip) * QUART, 16)
        att = jnp.concatenate(
            [att_scr[half, pl.ds(rows, QUART), :] for half in range(2)], axis=0
        )
        term = jnp.dot(att, w_ref[part], preferred_element_type=jnp.float32)
        out = term if out is None else out + term
    out_ref[...] = out.astype(jnp.bfloat16)


def per_device(queries, keys, values, block_of_slot, doc_lengths, out_weight):
    hbm = pl.BlockSpec(memory_space=pltpu.HBM)
    smem = pl.BlockSpec(memory_space=pltpu.SMEM)
    vmem = pl.BlockSpec(memory_space=pltpu.VMEM)
    spread = pl.pallas_call(
        spread_kernel,
        out_shape=jax.ShapeDtypeStruct((SRC, 4 * QUART, HD), jnp.bfloat16),
        in_specs=[hbm, hbm],
        out_specs=hbm,
        scratch_shapes=[
            pltpu.VMEM((4 * QUART, HD), jnp.bfloat16),
            pltpu.SemaphoreType.DMA((4,)),
            pltpu.SemaphoreType.DMA((SRC,)),
        ],
        name="spread",
    )(keys, values)
    spread, queries, out_weight = lax.optimization_barrier(
        (spread, queries, out_weight)
    )
    kv = lax.all_to_all(spread, KV_AXES, 0, 0, tiled=True)
    flip = [(0, 1), (1, 0)]
    q_side = lax.ppermute(queries, "xl", flip)
    w_side = lax.ppermute(out_weight, "zl", flip)
    q = jnp.concatenate([queries, q_side])
    q = lax.all_gather(q, ("zl", "core"), axis=0, tiled=True)
    q = q.reshape(4, 2, TOK, HD)
    w0 = jnp.stack([out_weight, w_side])
    w1 = lax.ppermute(w0, "core", flip)

    lane = np.arange(TILE)
    in_half = (lane % QUART) // 16 * 64 + lane // HALF * 16 + lane % 16
    i32 = jnp.int32
    rank, in_order, tiles, q_pos, q_start, q = pl.pallas_call(
        table_kernel,
        out_shape=(
            jax.ShapeDtypeStruct((PIECES + 1,), i32),
            jax.ShapeDtypeStruct((SLOTS,), i32),
            jax.ShapeDtypeStruct((4, 4), i32),
            jax.ShapeDtypeStruct((4, TILE), i32),
            jax.ShapeDtypeStruct((4, TILE), i32),
            jax.ShapeDtypeStruct((4, TILE, HD), jnp.bfloat16),
        ),
        in_specs=[smem, smem, vmem, vmem],
        out_specs=(smem, smem, smem, vmem, vmem, vmem),
        scratch_shapes=[
            pltpu.SMEM((2 * PIECES,), i32),
            pltpu.SMEM((2 * PIECES + 1,), i32),
        ],
        compiler_params=pltpu.CompilerParams(vmem_limit_bytes=8 << 20),
        name="tables",
    )(block_of_slot, doc_lengths, jnp.asarray(in_half[None, :], i32), q)
    kv, w1 = lax.optimization_barrier((kv, w1))

    sent = pl.pallas_call(
        attend_kernel,
        out_shape=jax.ShapeDtypeStruct((TEAM_SIZE, SEND, HD), jnp.bfloat16),
        in_specs=[smem, smem, smem, vmem, vmem, vmem, vmem],
        out_specs=vmem,
        scratch_shapes=[
            pltpu.VMEM((PAD, HD), jnp.int32),
            pltpu.VMEM((PAD, HD), jnp.bfloat16),
            pltpu.VMEM((PAD, HD), jnp.bfloat16),
            pltpu.VMEM((CHUNK, TILE), jnp.float32),
            pltpu.VMEM((1, TILE), jnp.float32),
            pltpu.VMEM((1, TILE), jnp.float32),
            pltpu.VMEM((HD, TILE), jnp.float32),
            pltpu.VMEM((TEAM_SIZE, STAT, HD), jnp.float32),
        ],
        compiler_params=pltpu.CompilerParams(vmem_limit_bytes=16 << 20),
        cost_estimate=pl.CostEstimate(
            flops=4 * 4 * TILE * KEYS * HD,
            transcendentals=4 * TILE * KEYS,
            bytes_accessed=4 << 20,
        ),
        name="attend",
    )(rank, in_order, tiles, kv, q, q_pos, q_start)
    got = lax.all_to_all(sent, TEAM, 0, 0, tiled=True)
    terms = pl.pallas_call(
        project_kernel,
        out_shape=jax.ShapeDtypeStruct((TOK // 4, out_weight.shape[1]), jnp.bfloat16),
        in_specs=[vmem, vmem, vmem],
        out_specs=vmem,
        scratch_shapes=[pltpu.VMEM((2, HALF, HD), jnp.bfloat16)],
        compiler_params=pltpu.CompilerParams(vmem_limit_bytes=16 << 20),
        name="project",
    )(got, w0, w1)
    parts = lax.all_to_all(terms.reshape(6, 16, -1), Z6, 0, 0, tiled=True)
    return jnp.sum(parts.astype(jnp.float32), axis=0).astype(jnp.bfloat16)


def solution(mesh):
    fine = Mesh(mesh.devices.reshape(SIZES), AXES)
    return jax.shard_map(
        per_device,
        mesh=fine,
        in_specs=(P(DP, HEAD), P(DP, None), P(DP, None), P(), P(), P(HEAD, None)),
        out_specs=P(DP + HEAD, None),
        check_vma=False,
    )
```

```python
import math

import jax
import jax.numpy as jnp
import numpy as np
from jax import lax
from jax.experimental import pallas as pl
from jax.experimental.pallas import tpu as pltpu
from jax.sharding import Mesh, PartitionSpec as P

AXES = ("y", "xh", "xl", "zh", "zm", "zl", "core")
SIZES = (8, 2, 2, 3, 2, 2, 2)
DP = ("y", "xh", "xl")
HEAD = ("zh", "zm", "zl", "core")
KV_AXES = ("y", "xh")
TEAM = ("xl", "zl", "core")
Z6 = ("zh", "zm")

TOK = 384
HALF = 192
HD = 128
QUART = 48
SRC = 16
PIECES = 2 * SRC
CHUNK = 256
KEYS = PIECES * QUART
PAD = KEYS + CHUNK
SLOTS = PIECES + CHUNK // QUART + 2
TILE = 4 * HALF
TEAM_SIZE = 8
STAT = 16
SEND = TOK + STAT
LOW = -1e30
FAR = 1 << 20
SCALE = math.log2(math.e) / math.sqrt(HD)


def spread_kernel(k_hbm, v_hbm, out_hbm, buf, in_sem, out_sem):
    own = lax.axis_index("zl") * 2 + lax.axis_index("core")
    row = pl.multiple_of(own * QUART, 16)
    col = pl.multiple_of(lax.axis_index("zh") * HD, HD)
    loads = []
    for n, src in enumerate((k_hbm, v_hbm)):
        for half in range(2):
            loads.append(
                pltpu.make_async_copy(
                    src.at[pl.ds(half * HALF + row, QUART), pl.ds(col, HD)],
                    buf.at[pl.ds((2 * n + half) * QUART, QUART), :],
                    in_sem.at[2 * n + half],
                )
            )
    for copy in loads:
        copy.start()
    for copy in loads:
        copy.wait()
    stores = [
        pltpu.make_async_copy(buf, out_hbm.at[n], out_sem.at[n]) for n in range(SRC)
    ]
    for copy in stores:
        copy.start()
    for copy in stores:
        copy.wait()


def start_of(pos, bounds):
    start = jnp.zeros_like(pos)
    for bound in bounds:
        start = jnp.where(pos >= bound, jnp.maximum(start, bound), start)
    return start


def table_kernel(
    slot_ref,
    len_ref,
    lane_ref,
    rank_ref,
    sorted_ref,
    tile_ref,
    qpos_ref,
    qstart_ref,
    where_scr,
    before_scr,
):
    xl = lax.axis_index("xl")
    here = lax.axis_index("y") * 2 + lax.axis_index("xh")

    def clear(n, carry):
        where_scr[n] = PIECES
        return carry

    lax.fori_loop(0, 2 * PIECES, clear, 0)
    for piece in range(PIECES):
        src, half = divmod(piece, 2)
        where_scr[slot_ref[4 * src + 2 * xl + half]] = piece

    def walk(block, count):
        before_scr[block] = count
        piece = where_scr[block]
        rank_ref[piece] = count
        sorted_ref[count] = block
        return count + (piece < PIECES).astype(jnp.int32)

    before_scr[2 * PIECES] = lax.fori_loop(0, 2 * PIECES, walk, jnp.int32(0))
    for n in range(PIECES, SLOTS):
        sorted_ref[n] = FAR // HALF
    bounds = [len_ref[0]]
    for n in range(1, len_ref.shape[0] - 1):
        bounds.append(bounds[-1] + len_ref[n])
    lane = lane_ref[...]
    for tile in range(4):
        rel, half = divmod(tile, 2)
        block = slot_ref[4 * here + 2 * (xl ^ rel) + half]
        base = block * HALF
        low = before_scr[lax.div(start_of(base, bounds), HALF)]
        high = before_scr[block + 1]
        tile_ref[tile, 0] = low
        tile_ref[tile, 1] = lax.div((high - low) * QUART + CHUNK - 1, CHUNK)
        tile_ref[tile, 2] = base
        tile_ref[tile, 3] = start_of(base + HALF - 1, bounds)
        pos = lane + base
        qpos_ref[tile : tile + 1, :] = pos
        qstart_ref[tile : tile + 1, :] = start_of(pos, bounds)


def attend_kernel(
    rank_ref,
    sorted_ref,
    tile_ref,
    kv_ref,
    q_own_ref,
    q_side_ref,
    qpos_ref,
    qstart_ref,
    out_ref,
    kpos_scr,
    k_scr,
    v_scr,
    q_scr,
    s_scr,
    m_scr,
    l_scr,
    acc_scr,
    st_scr,
):
    for piece in range(PIECES):
        src, half = divmod(piece, 2)
        at = pl.multiple_of(rank_ref[piece] * QUART, 16)
        k_scr[pl.ds(at, QUART), :] = kv_ref[src, half * QUART : (half + 1) * QUART, :]
        v_scr[pl.ds(at, QUART), :] = kv_ref[
            src, (2 + half) * QUART : (3 + half) * QUART, :
        ]
    k_scr[KEYS:, :] = jnp.zeros((CHUNK, HD), jnp.bfloat16)
    v_scr[KEYS:, :] = jnp.zeros((CHUNK, HD), jnp.bfloat16)
    st_scr[...] = jnp.zeros_like(st_scr)
    own = lax.axis_index("zl") * 2 + lax.axis_index("core")
    row = lax.broadcasted_iota(jnp.int32, (QUART, HD), 0) + own * QUART
    for n in range(PIECES):
        kpos_scr[n * QUART : (n + 1) * QUART, :] = row + sorted_ref[n] * HALF
    kpos_scr[KEYS:, :] = jnp.full((PAD - KEYS, HD), FAR, jnp.int32)

    for tile in range(4):
        q_ref = (q_own_ref, q_side_ref)[tile // 2]
        half = tile % 2
        for d in range(4):
            for j in range(4):
                for z3 in range(3):
                    to = d * HALF + j * QUART + z3 * 16
                    of = j * TOK + half * HALF + z3 * 64 + d * 16
                    q_scr[tile, to : to + 16, :] = q_ref[of : of + 16, :]

    def one_tile(tile, carry):
        low, steps, q_first, start_last = (tile_ref[tile, n] for n in range(4))
        m_scr[...] = jnp.full_like(m_scr, LOW)
        l_scr[...] = jnp.zeros_like(l_scr)
        acc_scr[...] = jnp.zeros_like(acc_scr)

        def one_step(step, carry):
            first = low * QUART + step * CHUNK
            at = pl.multiple_of(first, 16)
            s_scr[...] = lax.dot_general(
                k_scr[pl.ds(at, CHUNK), :],
                q_scr[tile],
                (((1,), (1,)), ((), ())),
                preferred_element_type=jnp.float32,
            )
            first_pos = sorted_ref[lax.div(first, QUART)] * HALF
            last_pos = sorted_ref[lax.div(first + CHUNK - 1, QUART)] * HALF + HALF - 1

            @pl.when((last_pos > q_first) | (first_pos < start_last))
            def _():
                key_pos = kpos_scr[pl.ds(at, CHUNK), :]
                key_pos = jnp.concatenate([key_pos] * (TILE // HD), axis=1)
                allowed = (key_pos <= qpos_ref[pl.ds(tile, 1), :]) & (
                    key_pos >= qstart_ref[pl.ds(tile, 1), :]
                )
                s_scr[...] = jnp.where(allowed, s_scr[...], LOW)

            scores = s_scr[...]
            old = m_scr[...]
            new = jnp.maximum(old, jnp.max(scores, axis=0, keepdims=True))
            m_scr[...] = new
            probs = jnp.exp2((scores - new) * SCALE)
            factor = jnp.exp2((old - new) * SCALE)
            l_scr[...] = l_scr[...] * factor + jnp.sum(probs, axis=0, keepdims=True)
            acc_scr[...] = acc_scr[...] * factor + lax.dot_general(
                v_scr[pl.ds(at, CHUNK), :],
                probs.astype(jnp.bfloat16),
                (((0,), (0,)), ((), ())),
                preferred_element_type=jnp.float32,
            )
            return carry

        lax.fori_loop(0, steps, one_step, 0)
        total = jnp.where(l_scr[...] > 0, l_scr[...], 1.0)
        part = (acc_scr[...] / total).T.astype(jnp.bfloat16)
        lse = m_scr[...] * SCALE + jnp.log2(total)
        high = lse.astype(jnp.bfloat16).astype(jnp.float32)
        mid = (lse - high).astype(jnp.bfloat16).astype(jnp.float32)
        stats = (high, mid, lse - high - mid)
        xl4 = ((tile >> 1) ^ lax.axis_index("xl")) * 4
        half = tile & 1
        rows = pl.multiple_of(half * HALF, 16)
        for d in range(4):
            out_ref[xl4 + d, pl.ds(rows, HALF), :] = part[d * HALF : (d + 1) * HALF]
            for n, stat in enumerate(stats):
                if d % 2:
                    stat = pltpu.roll(
                        jnp.broadcast_to(stat, (8, TILE)), TILE - 64, 1
                    )[:1]
                base = d * HALF - (d % 2) * 64
                for w in range(2):
                    st_scr[xl4 + d, pl.ds(half * 6 + n * 2 + w, 1), :] = stat[
                        :, base + w * 128 : base + (w + 1) * 128
                    ]
        return carry

    lax.fori_loop(0, 4, one_tile, 0)
    for dest in range(TEAM_SIZE):
        out_ref[dest, TOK:, :] = st_scr[dest].astype(jnp.bfloat16)


def project_kernel(got_ref, w0_ref, w1_ref, out_ref, att_scr):
    for half in range(2):
        sides = []
        for w in range(2):
            lse = []
            for k in range(TEAM_SIZE):
                stat = got_ref[k, TOK:, :].astype(jnp.float32)
                row = half * 6 + w
                lse.append(
                    stat[row : row + 1] + stat[row + 2 : row + 3] + stat[row + 4 : row + 5]
                )
            lse = jnp.concatenate(lse, axis=0)
            weight = jnp.exp2(lse - jnp.max(lse, axis=0, keepdims=True))
            weight = weight / jnp.sum(weight, axis=0, keepdims=True)
            sides.append(weight.T)
        weight = jnp.concatenate([sides[0], sides[1][:64]], axis=0)
        total = jnp.zeros((HALF, HD), jnp.float32)
        for k in range(TEAM_SIZE):
            total += weight[:, k : k + 1] * got_ref[
                k, half * HALF : (half + 1) * HALF, :
            ].astype(jnp.float32)
        att_scr[half] = total.astype(jnp.bfloat16)
    own = lax.axis_index("zl") * 2 + lax.axis_index("core")
    out = None
    for w_ref, part, flip in ((w0_ref, 0, 0), (w0_ref, 1, 2), (w1_ref, 0, 1), (w1_ref, 1, 3)):
        rows = pl.multiple_of((own ^ flip) * QUART, 16)
        att = jnp.concatenate(
            [att_scr[half, pl.ds(rows, QUART), :] for half in range(2)], axis=0
        )
        term = jnp.dot(att, w_ref[part], preferred_element_type=jnp.float32)
        out = term if out is None else out + term
    out_ref[...] = out.astype(jnp.bfloat16)


def per_device(queries, keys, values, block_of_slot, doc_lengths, out_weight):
    hbm = pl.BlockSpec(memory_space=pltpu.HBM)
    smem = pl.BlockSpec(memory_space=pltpu.SMEM)
    vmem = pl.BlockSpec(memory_space=pltpu.VMEM)
    spread = pl.pallas_call(
        spread_kernel,
        out_shape=jax.ShapeDtypeStruct((SRC, 4 * QUART, HD), jnp.bfloat16),
        in_specs=[hbm, hbm],
        out_specs=hbm,
        scratch_shapes=[
            pltpu.VMEM((4 * QUART, HD), jnp.bfloat16),
            pltpu.SemaphoreType.DMA((4,)),
            pltpu.SemaphoreType.DMA((SRC,)),
        ],
        name="spread",
    )(keys, values)
    spread, queries, out_weight = lax.optimization_barrier(
        (spread, queries, out_weight)
    )
    kv = lax.all_to_all(spread, KV_AXES, 0, 0, tiled=True)
    flip = [(0, 1), (1, 0)]
    q = lax.all_gather(queries, ("zl", "core"), axis=0, tiled=True)
    q_side = lax.ppermute(q, "xl", flip)
    w_side = lax.ppermute(out_weight, "zl", flip)
    w0 = jnp.stack([out_weight, w_side])
    w1 = lax.ppermute(w0, "core", flip)

    lane = np.arange(TILE)
    in_half = (lane % QUART) // 16 * 64 + lane // HALF * 16 + lane % 16
    i32 = jnp.int32
    rank, in_order, tiles, q_pos, q_start = pl.pallas_call(
        table_kernel,
        out_shape=(
            jax.ShapeDtypeStruct((PIECES + 1,), i32),
            jax.ShapeDtypeStruct((SLOTS,), i32),
            jax.ShapeDtypeStruct((4, 4), i32),
            jax.ShapeDtypeStruct((4, TILE), i32),
            jax.ShapeDtypeStruct((4, TILE), i32),
        ),
        in_specs=[smem, smem, vmem],
        out_specs=(smem, smem, smem, vmem, vmem),
        scratch_shapes=[
            pltpu.SMEM((2 * PIECES,), i32),
            pltpu.SMEM((2 * PIECES + 1,), i32),
        ],
        compiler_params=pltpu.CompilerParams(vmem_limit_bytes=8 << 20),
        name="tables",
    )(block_of_slot, doc_lengths, jnp.asarray(in_half[None, :], i32))
    kv, w1 = lax.optimization_barrier((kv, w1))

    sent = pl.pallas_call(
        attend_kernel,
        out_shape=jax.ShapeDtypeStruct((TEAM_SIZE, SEND, HD), jnp.bfloat16),
        in_specs=[smem, smem, smem, vmem, vmem, vmem, vmem, vmem],
        out_specs=vmem,
        scratch_shapes=[
            pltpu.VMEM((PAD, HD), jnp.int32),
            pltpu.VMEM((PAD, HD), jnp.bfloat16),
            pltpu.VMEM((PAD, HD), jnp.bfloat16),
            pltpu.VMEM((4, TILE, HD), jnp.bfloat16),
            pltpu.VMEM((CHUNK, TILE), jnp.float32),
            pltpu.VMEM((1, TILE), jnp.float32),
            pltpu.VMEM((1, TILE), jnp.float32),
            pltpu.VMEM((HD, TILE), jnp.float32),
            pltpu.VMEM((TEAM_SIZE, STAT, HD), jnp.float32),
        ],
        compiler_params=pltpu.CompilerParams(vmem_limit_bytes=16 << 20),
        cost_estimate=pl.CostEstimate(
            flops=4 * 4 * TILE * KEYS * HD,
            transcendentals=4 * TILE * KEYS,
            bytes_accessed=4 << 20,
        ),
        name="attend",
    )(rank, in_order, tiles, kv, q, q_side, q_pos, q_start)
    got = lax.all_to_all(sent, TEAM, 0, 0, tiled=True)
    terms = pl.pallas_call(
        project_kernel,
        out_shape=jax.ShapeDtypeStruct((TOK // 4, out_weight.shape[1]), jnp.bfloat16),
        in_specs=[vmem, vmem, vmem],
        out_specs=vmem,
        scratch_shapes=[pltpu.VMEM((2, HALF, HD), jnp.bfloat16)],
        compiler_params=pltpu.CompilerParams(vmem_limit_bytes=16 << 20),
        name="project",
    )(got, w0, w1)
    parts = lax.all_to_all(terms.reshape(6, 16, -1), Z6, 0, 0, tiled=True)
    return jnp.sum(parts.astype(jnp.float32), axis=0).astype(jnp.bfloat16)


def solution(mesh):
    fine = Mesh(mesh.devices.reshape(SIZES), AXES)
    return jax.shard_map(
        per_device,
        mesh=fine,
        in_specs=(P(DP, HEAD), P(DP, None), P(DP, None), P(), P(), P(HEAD, None)),
        out_specs=P(DP + HEAD, None),
        check_vma=False,
    )
```

```python
import math

import jax
import jax.numpy as jnp
import numpy as np
from jax import lax
from jax.experimental import pallas as pl
from jax.experimental.pallas import tpu as pltpu
from jax.sharding import Mesh, PartitionSpec as P

AXES = ("y", "xh", "xl", "zh", "zm", "zl", "core")
SIZES = (8, 2, 2, 3, 2, 2, 2)
DP = ("y", "xh", "xl")
HEAD = ("zh", "zm", "zl", "core")
KV_AXES = ("y", "xh")
TEAM = ("xl", "zl", "core")
Z6 = ("zh", "zm")

TOK = 384
HALF = 192
HD = 128
QUART = 48
SRC = 16
PIECES = 2 * SRC
CHUNK = 256
KEYS = PIECES * QUART
PAD = KEYS + CHUNK
SLOTS = PIECES + CHUNK // QUART + 2
TILE = 4 * HALF
TEAM_SIZE = 8
STAT = 16
SEND = TOK + STAT
LOW = -1e30
FAR = 1 << 20
SCALE = math.log2(math.e) / math.sqrt(HD)


def spread_kernel(k_hbm, v_hbm, out_hbm, buf, in_sem, out_sem):
    own = lax.axis_index("zl") * 2 + lax.axis_index("core")
    row = pl.multiple_of(own * QUART, 16)
    col = pl.multiple_of(lax.axis_index("zh") * HD, HD)
    loads = []
    for n, src in enumerate((k_hbm, v_hbm)):
        for half in range(2):
            loads.append(
                pltpu.make_async_copy(
                    src.at[pl.ds(half * HALF + row, QUART), pl.ds(col, HD)],
                    buf.at[pl.ds((2 * n + half) * QUART, QUART), :],
                    in_sem.at[2 * n + half],
                )
            )
    for copy in loads:
        copy.start()
    for copy in loads:
        copy.wait()
    stores = [
        pltpu.make_async_copy(buf, out_hbm.at[n], out_sem.at[n]) for n in range(SRC)
    ]
    for copy in stores:
        copy.start()
    for copy in stores:
        copy.wait()


def start_of(pos, bounds):
    start = jnp.zeros_like(pos)
    for bound in bounds:
        start = jnp.where(pos >= bound, jnp.maximum(start, bound), start)
    return start


def table_kernel(
    slot_ref,
    len_ref,
    lane_ref,
    rank_ref,
    sorted_ref,
    tile_ref,
    qpos_ref,
    qstart_ref,
    where_scr,
    before_scr,
):
    xl = lax.axis_index("xl")
    here = lax.axis_index("y") * 2 + lax.axis_index("xh")

    def clear(n, carry):
        where_scr[n] = PIECES
        return carry

    lax.fori_loop(0, 2 * PIECES, clear, 0)
    for piece in range(PIECES):
        src, half = divmod(piece, 2)
        where_scr[slot_ref[4 * src + 2 * xl + half]] = piece

    def walk(block, count):
        before_scr[block] = count
        piece = where_scr[block]
        rank_ref[piece] = count
        sorted_ref[count] = block
        return count + (piece < PIECES).astype(jnp.int32)

    before_scr[2 * PIECES] = lax.fori_loop(0, 2 * PIECES, walk, jnp.int32(0))
    for n in range(PIECES, SLOTS):
        sorted_ref[n] = FAR // HALF
    bounds = [len_ref[0]]
    for n in range(1, len_ref.shape[0] - 1):
        bounds.append(bounds[-1] + len_ref[n])
    lane = lane_ref[...]
    for tile in range(4):
        rel, half = divmod(tile, 2)
        block = slot_ref[4 * here + 2 * (xl ^ rel) + half]
        base = block * HALF
        low = before_scr[lax.div(start_of(base, bounds), HALF)]
        high = before_scr[block + 1]
        tile_ref[tile, 0] = low
        tile_ref[tile, 1] = lax.div((high - low) * QUART + CHUNK - 1, CHUNK)
        tile_ref[tile, 2] = base
        tile_ref[tile, 3] = start_of(base + HALF - 1, bounds)
        pos = lane + base
        qpos_ref[tile : tile + 1, :] = pos
        qstart_ref[tile : tile + 1, :] = start_of(pos, bounds)


def attend_kernel(
    rank_ref,
    sorted_ref,
    tile_ref,
    kv_ref,
    q_own_ref,
    q_side_ref,
    qpos_ref,
    qstart_ref,
    out_ref,
    kpos_scr,
    k_scr,
    v_scr,
    q_scr,
    s_scr,
    m_scr,
    l_scr,
    acc_scr,
    st_scr,
):
    for piece in range(PIECES):
        src, half = divmod(piece, 2)
        at = pl.multiple_of(rank_ref[piece] * QUART, 16)
        k_scr[pl.ds(at, QUART), :] = kv_ref[src, half * QUART : (half + 1) * QUART, :]
        v_scr[pl.ds(at, QUART), :] = kv_ref[
            src, (2 + half) * QUART : (3 + half) * QUART, :
        ]
    k_scr[KEYS:, :] = jnp.zeros((CHUNK, HD), jnp.bfloat16)
    v_scr[KEYS:, :] = jnp.zeros((CHUNK, HD), jnp.bfloat16)
    st_scr[...] = jnp.zeros_like(st_scr)
    own = lax.axis_index("zl") * 2 + lax.axis_index("core")
    row = lax.broadcasted_iota(jnp.int32, (QUART, HD), 0) + own * QUART
    for n in range(PIECES):
        kpos_scr[n * QUART : (n + 1) * QUART, :] = row + sorted_ref[n] * HALF
    kpos_scr[KEYS:, :] = jnp.full((PAD - KEYS, HD), FAR, jnp.int32)

    for tile in range(4):
        q_ref = (q_own_ref, q_side_ref)[tile // 2]
        half = tile % 2
        for d in range(4):
            for j in range(4):
                for z3 in range(3):
                    to = d * HALF + j * QUART + z3 * 16
                    of = j * TOK + half * HALF + z3 * 64 + d * 16
                    q_scr[tile, to : to + 16, :] = q_ref[of : of + 16, :]

    def one_tile(tile, carry):
        low, steps, q_first, start_last = (tile_ref[tile, n] for n in range(4))
        m_scr[...] = jnp.full_like(m_scr, LOW)
        l_scr[...] = jnp.zeros_like(l_scr)
        acc_scr[...] = jnp.zeros_like(acc_scr)

        def one_step(step, carry):
            first = low * QUART + step * CHUNK
            at = pl.multiple_of(first, 16)
            s_scr[...] = lax.dot_general(
                k_scr[pl.ds(at, CHUNK), :],
                q_scr[tile],
                (((1,), (1,)), ((), ())),
                preferred_element_type=jnp.float32,
            )
            first_pos = sorted_ref[lax.div(first, QUART)] * HALF
            last_pos = sorted_ref[lax.div(first + CHUNK - 1, QUART)] * HALF + HALF - 1

            @pl.when((last_pos > q_first) | (first_pos < start_last))
            def _():
                key_pos = kpos_scr[pl.ds(at, CHUNK), :]
                key_pos = jnp.concatenate([key_pos] * (TILE // HD), axis=1)
                allowed = (key_pos <= qpos_ref[pl.ds(tile, 1), :]) & (
                    key_pos >= qstart_ref[pl.ds(tile, 1), :]
                )
                s_scr[...] = jnp.where(allowed, s_scr[...], LOW)

            scores = s_scr[...]
            old = m_scr[...]
            new = jnp.maximum(old, jnp.max(scores, axis=0, keepdims=True))
            m_scr[...] = new
            probs = jnp.exp2((scores - new) * SCALE)
            factor = jnp.exp2((old - new) * SCALE)
            l_scr[...] = l_scr[...] * factor + jnp.sum(probs, axis=0, keepdims=True)
            acc_scr[...] = acc_scr[...] * factor + lax.dot_general(
                v_scr[pl.ds(at, CHUNK), :],
                probs.astype(jnp.bfloat16),
                (((0,), (0,)), ((), ())),
                preferred_element_type=jnp.float32,
            )
            return carry

        lax.fori_loop(0, steps, one_step, 0)
        total = jnp.where(l_scr[...] > 0, l_scr[...], 1.0)
        part = (acc_scr[...] / total).T.astype(jnp.bfloat16)
        lse = m_scr[...] * SCALE + jnp.log2(total)
        high = lse.astype(jnp.bfloat16).astype(jnp.float32)
        mid = (lse - high).astype(jnp.bfloat16).astype(jnp.float32)
        stats = (high, mid, lse - high - mid)
        xl4 = ((tile >> 1) ^ lax.axis_index("xl")) * 4
        half = tile & 1
        rows = pl.multiple_of(half * HALF, 16)
        for d in range(4):
            out_ref[xl4 + d, pl.ds(rows, HALF), :] = part[d * HALF : (d + 1) * HALF]
            for n, stat in enumerate(stats):
                if d % 2:
                    stat = pltpu.roll(
                        jnp.broadcast_to(stat, (8, TILE)), TILE - 64, 1
                    )[:1]
                base = d * HALF - (d % 2) * 64
                for w in range(2):
                    st_scr[xl4 + d, pl.ds(half * 6 + n * 2 + w, 1), :] = stat[
                        :, base + w * 128 : base + (w + 1) * 128
                    ]
        return carry

    lax.fori_loop(0, 4, one_tile, 0)
    for dest in range(TEAM_SIZE):
        out_ref[dest, TOK:, :] = st_scr[dest].astype(jnp.bfloat16)


def project_kernel(got_ref, w0_ref, w1_ref, out_ref, att_scr):
    for half in range(2):
        sides = []
        for w in range(2):
            lse = []
            for k in range(TEAM_SIZE):
                stat = got_ref[k, TOK:, :].astype(jnp.float32)
                row = half * 6 + w
                lse.append(
                    stat[row : row + 1] + stat[row + 2 : row + 3] + stat[row + 4 : row + 5]
                )
            lse = jnp.concatenate(lse, axis=0)
            weight = jnp.exp2(lse - jnp.max(lse, axis=0, keepdims=True))
            weight = weight / jnp.sum(weight, axis=0, keepdims=True)
            sides.append(weight.T)
        weight = jnp.concatenate([sides[0], sides[1][:64]], axis=0)
        total = jnp.zeros((HALF, HD), jnp.float32)
        for k in range(TEAM_SIZE):
            total += weight[:, k : k + 1] * got_ref[
                k, half * HALF : (half + 1) * HALF, :
            ].astype(jnp.float32)
        att_scr[half] = total.astype(jnp.bfloat16)
    own = lax.axis_index("zl") * 2 + lax.axis_index("core")
    out = None
    for w_ref, part, flip in ((w0_ref, 0, 0), (w0_ref, 1, 2), (w1_ref, 0, 1), (w1_ref, 1, 3)):
        rows = pl.multiple_of((own ^ flip) * QUART, 16)
        att = jnp.concatenate(
            [att_scr[half, pl.ds(rows, QUART), :] for half in range(2)], axis=0
        )
        term = jnp.dot(att, w_ref[part], preferred_element_type=jnp.float32)
        out = term if out is None else out + term
    out_ref[...] = out.astype(jnp.bfloat16)


def per_device(queries, keys, values, block_of_slot, doc_lengths, out_weight):
    hbm = pl.BlockSpec(memory_space=pltpu.HBM)
    smem = pl.BlockSpec(memory_space=pltpu.SMEM)
    vmem = pl.BlockSpec(memory_space=pltpu.VMEM)
    spread = pl.pallas_call(
        spread_kernel,
        out_shape=jax.ShapeDtypeStruct((SRC, 4 * QUART, HD), jnp.bfloat16),
        in_specs=[hbm, hbm],
        out_specs=hbm,
        scratch_shapes=[
            pltpu.VMEM((4 * QUART, HD), jnp.bfloat16),
            pltpu.SemaphoreType.DMA((4,)),
            pltpu.SemaphoreType.DMA((SRC,)),
        ],
        name="spread",
    )(keys, values)
    spread, queries, out_weight = lax.optimization_barrier(
        (spread, queries, out_weight)
    )
    kv = lax.all_to_all(spread, KV_AXES, 0, 0, tiled=True)
    flip = [(0, 1), (1, 0)]
    q_side = lax.ppermute(queries, "xl", flip)
    q = lax.all_gather(queries, ("zl", "core"), axis=0, tiled=True)
    q_side = lax.all_gather(q_side, ("zl", "core"), axis=0, tiled=True)
    w_side = lax.ppermute(out_weight, "zl", flip)

    lane = np.arange(TILE)
    in_half = (lane % QUART) // 16 * 64 + lane // HALF * 16 + lane % 16
    i32 = jnp.int32
    rank, in_order, tiles, q_pos, q_start = pl.pallas_call(
        table_kernel,
        out_shape=(
            jax.ShapeDtypeStruct((PIECES + 1,), i32),
            jax.ShapeDtypeStruct((SLOTS,), i32),
            jax.ShapeDtypeStruct((4, 4), i32),
            jax.ShapeDtypeStruct((4, TILE), i32),
            jax.ShapeDtypeStruct((4, TILE), i32),
        ),
        in_specs=[smem, smem, vmem],
        out_specs=(smem, smem, smem, vmem, vmem),
        scratch_shapes=[
            pltpu.SMEM((2 * PIECES,), i32),
            pltpu.SMEM((2 * PIECES + 1,), i32),
        ],
        compiler_params=pltpu.CompilerParams(vmem_limit_bytes=8 << 20),
        name="tables",
    )(block_of_slot, doc_lengths, jnp.asarray(in_half[None, :], i32))

    sent = pl.pallas_call(
        attend_kernel,
        out_shape=jax.ShapeDtypeStruct((TEAM_SIZE, SEND, HD), jnp.bfloat16),
        in_specs=[smem, smem, smem, vmem, vmem, vmem, vmem, vmem],
        out_specs=vmem,
        scratch_shapes=[
            pltpu.VMEM((PAD, HD), jnp.int32),
            pltpu.VMEM((PAD, HD), jnp.bfloat16),
            pltpu.VMEM((PAD, HD), jnp.bfloat16),
            pltpu.VMEM((4, TILE, HD), jnp.bfloat16),
            pltpu.VMEM((CHUNK, TILE), jnp.float32),
            pltpu.VMEM((1, TILE), jnp.float32),
            pltpu.VMEM((1, TILE), jnp.float32),
            pltpu.VMEM((HD, TILE), jnp.float32),
            pltpu.VMEM((TEAM_SIZE, STAT, HD), jnp.float32),
        ],
        compiler_params=pltpu.CompilerParams(vmem_limit_bytes=16 << 20),
        cost_estimate=pl.CostEstimate(
            flops=4 * 4 * TILE * KEYS * HD,
            transcendentals=4 * TILE * KEYS,
            bytes_accessed=4 << 20,
        ),
        name="attend",
    )(rank, in_order, tiles, kv, q, q_side, q_pos, q_start)
    sent, w_side = lax.optimization_barrier((sent, w_side))
    got = lax.all_to_all(sent, TEAM, 0, 0, tiled=True)
    w0 = jnp.stack([out_weight, w_side])
    w1 = lax.ppermute(w0, "core", flip)
    terms = pl.pallas_call(
        project_kernel,
        out_shape=jax.ShapeDtypeStruct((TOK // 4, out_weight.shape[1]), jnp.bfloat16),
        in_specs=[vmem, vmem, vmem],
        out_specs=vmem,
        scratch_shapes=[pltpu.VMEM((2, HALF, HD), jnp.bfloat16)],
        compiler_params=pltpu.CompilerParams(vmem_limit_bytes=16 << 20),
        name="project",
    )(got, w0, w1)
    parts = lax.all_to_all(terms.reshape(6, 16, -1), Z6, 0, 0, tiled=True)
    return jnp.sum(parts.astype(jnp.float32), axis=0).astype(jnp.bfloat16)


def solution(mesh):
    fine = Mesh(mesh.devices.reshape(SIZES), AXES)
    return jax.shard_map(
        per_device,
        mesh=fine,
        in_specs=(P(DP, HEAD), P(DP, None), P(DP, None), P(), P(), P(HEAD, None)),
        out_specs=P(DP + HEAD, None),
        check_vma=False,
    )
```

```python
import math

import jax
import jax.numpy as jnp
import numpy as np
from jax import lax
from jax.experimental import pallas as pl
from jax.experimental.pallas import tpu as pltpu
from jax.sharding import Mesh, PartitionSpec as P

AXES = ("y", "xh", "xl", "zh", "zm", "zl", "core")
SIZES = (8, 2, 2, 3, 2, 2, 2)
DP = ("y", "xh", "xl")
HEAD = ("zh", "zm", "zl", "core")
KV_AXES = ("y", "xh")
TEAM = ("xl", "zl", "core")
Z6 = ("zh", "zm")

TOK = 384
HALF = 192
HD = 128
QUART = 48
SRC = 16
PIECES = 2 * SRC
CHUNK = 256
KEYS = PIECES * QUART
PAD = KEYS + CHUNK
SLOTS = PIECES + CHUNK // QUART + 2
TILE = 4 * HALF
LANES = 384
TEAM_SIZE = 8
STAT = 16
SEND = TOK + STAT
LOW = -1e30
FAR = 1 << 20
SCALE = math.log2(math.e) / math.sqrt(HD)


def spread_kernel(k_hbm, v_hbm, out_hbm, buf, in_sem, out_sem):
    own = lax.axis_index("zl") * 2 + lax.axis_index("core")
    row = pl.multiple_of(own * QUART, 16)
    col = pl.multiple_of(lax.axis_index("zh") * HD, HD)
    loads = []
    for n, src in enumerate((k_hbm, v_hbm)):
        for half in range(2):
            loads.append(
                pltpu.make_async_copy(
                    src.at[pl.ds(half * HALF + row, QUART), pl.ds(col, HD)],
                    buf.at[pl.ds((2 * n + half) * QUART, QUART), :],
                    in_sem.at[2 * n + half],
                )
            )
    for copy in loads:
        copy.start()
    for copy in loads:
        copy.wait()
    stores = [
        pltpu.make_async_copy(buf, out_hbm.at[n], out_sem.at[n]) for n in range(SRC)
    ]
    for copy in stores:
        copy.start()
    for copy in stores:
        copy.wait()


def start_of(pos, bounds):
    start = jnp.zeros_like(pos)
    for bound in bounds:
        start = jnp.where(pos >= bound, jnp.maximum(start, bound), start)
    return start


def table_kernel(
    slot_ref,
    len_ref,
    lane_ref,
    rank_ref,
    sorted_ref,
    tile_ref,
    qpos_ref,
    qstart_ref,
    where_scr,
    before_scr,
):
    xl = lax.axis_index("xl")
    here = lax.axis_index("y") * 2 + lax.axis_index("xh")

    def clear(n, carry):
        where_scr[n] = PIECES
        return carry

    lax.fori_loop(0, 2 * PIECES, clear, 0)
    for piece in range(PIECES):
        src, half = divmod(piece, 2)
        where_scr[slot_ref[4 * src + 2 * xl + half]] = piece

    def walk(block, count):
        before_scr[block] = count
        piece = where_scr[block]
        rank_ref[piece] = count
        sorted_ref[count] = block
        return count + (piece < PIECES).astype(jnp.int32)

    before_scr[2 * PIECES] = lax.fori_loop(0, 2 * PIECES, walk, jnp.int32(0))
    for n in range(PIECES, SLOTS):
        sorted_ref[n] = FAR // HALF
    bounds = [len_ref[0]]
    for n in range(1, len_ref.shape[0] - 1):
        bounds.append(bounds[-1] + len_ref[n])
    lane = lane_ref[...]
    for tile in range(4):
        rel, half = divmod(tile, 2)
        block = slot_ref[4 * here + 2 * (xl ^ rel) + half]
        base = block * HALF
        low = before_scr[lax.div(start_of(base, bounds), HALF)]
        high = before_scr[block + 1]
        tile_ref[tile, 0] = low
        tile_ref[tile, 1] = lax.div((high - low) * QUART + CHUNK - 1, CHUNK)
        tile_ref[tile, 2] = base
        tile_ref[tile, 3] = start_of(base + HALF - 1, bounds)
        pos = lane + base
        qpos_ref[tile : tile + 1, :] = pos
        qstart_ref[tile : tile + 1, :] = start_of(pos, bounds)


def attend_kernel(
    rank_ref,
    sorted_ref,
    tile_ref,
    kv_ref,
    q_own_ref,
    q_side_ref,
    qpos_ref,
    qstart_ref,
    out_ref,
    kpos_scr,
    k_scr,
    v_scr,
    q_scr,
    m_scr,
    l_scr,
    acc_scr,
    st_scr,
):
    for piece in range(PIECES):
        src, half = divmod(piece, 2)
        at = pl.multiple_of(rank_ref[piece] * QUART, 16)
        k_scr[pl.ds(at, QUART), :] = kv_ref[src, half * QUART : (half + 1) * QUART, :]
        v_scr[pl.ds(at, QUART), :] = kv_ref[
            src, (2 + half) * QUART : (3 + half) * QUART, :
        ]
    k_scr[KEYS:, :] = jnp.zeros((CHUNK, HD), jnp.bfloat16)
    v_scr[KEYS:, :] = jnp.zeros((CHUNK, HD), jnp.bfloat16)
    st_scr[...] = jnp.zeros_like(st_scr)
    own = lax.axis_index("zl") * 2 + lax.axis_index("core")
    row = lax.broadcasted_iota(jnp.int32, (QUART, HD), 0) + own * QUART
    for n in range(PIECES):
        kpos_scr[n * QUART : (n + 1) * QUART, :] = row + sorted_ref[n] * HALF
    kpos_scr[KEYS:, :] = jnp.full((PAD - KEYS, HD), FAR, jnp.int32)

    for tile in range(4):
        q_ref = (q_own_ref, q_side_ref)[tile // 2]
        half = tile % 2
        for d in range(4):
            for j in range(4):
                for z3 in range(3):
                    to = d * HALF + j * QUART + z3 * 16
                    of = j * TOK + half * HALF + z3 * 64 + d * 16
                    q_scr[tile, to : to + 16, :] = q_ref[of : of + 16, :]

    def one_tile(tile, carry):
        low, steps, q_first, start_last = (tile_ref[tile, n] for n in range(4))
        m_scr[...] = jnp.full_like(m_scr, LOW)
        l_scr[...] = jnp.zeros_like(l_scr)
        acc_scr[...] = jnp.zeros_like(acc_scr)

        def one_step(step, carry):
            first = low * QUART + step * CHUNK
            at = pl.multiple_of(first, 16)
            first_pos = sorted_ref[lax.div(first, QUART)] * HALF
            last_pos = sorted_ref[lax.div(first + CHUNK - 1, QUART)] * HALF + HALF - 1
            edge = (last_pos > q_first) | (first_pos < start_last)

            def block(masked):
                keys = k_scr[pl.ds(at, CHUNK), :]
                vals = v_scr[pl.ds(at, CHUNK), :]
                for part in range(TILE // LANES):
                    cols = slice(part * LANES, (part + 1) * LANES)
                    scores = lax.dot_general(
                        keys,
                        q_scr[tile, cols, :],
                        (((1,), (1,)), ((), ())),
                        preferred_element_type=jnp.float32,
                    )
                    if masked:
                        key_pos = kpos_scr[pl.ds(at, CHUNK), :]
                        key_pos = jnp.concatenate([key_pos] * (LANES // HD), axis=1)
                        allowed = (key_pos <= qpos_ref[pl.ds(tile, 1), cols]) & (
                            key_pos >= qstart_ref[pl.ds(tile, 1), cols]
                        )
                        scores = jnp.where(allowed, scores, LOW)
                    old = m_scr[:, cols]
                    new = jnp.maximum(old, jnp.max(scores, axis=0, keepdims=True))
                    m_scr[:, cols] = new
                    probs = jnp.exp2((scores - new) * SCALE)
                    factor = jnp.exp2((old - new) * SCALE)
                    l_scr[:, cols] = l_scr[:, cols] * factor + jnp.sum(
                        probs, axis=0, keepdims=True
                    )
                    acc_scr[:, cols] = acc_scr[:, cols] * factor + lax.dot_general(
                        vals,
                        probs.astype(jnp.bfloat16),
                        (((0,), (0,)), ((), ())),
                        preferred_element_type=jnp.float32,
                    )

            pl.when(edge)(lambda: block(True))
            pl.when(jnp.logical_not(edge))(lambda: block(False))
            return carry

        lax.fori_loop(0, steps, one_step, 0)
        total = jnp.where(l_scr[...] > 0, l_scr[...], 1.0)
        part = (acc_scr[...] / total).T.astype(jnp.bfloat16)
        lse = m_scr[...] * SCALE + jnp.log2(total)
        high = lse.astype(jnp.bfloat16).astype(jnp.float32)
        mid = (lse - high).astype(jnp.bfloat16).astype(jnp.float32)
        stats = (high, mid, lse - high - mid)
        xl4 = ((tile >> 1) ^ lax.axis_index("xl")) * 4
        half = tile & 1
        rows = pl.multiple_of(half * HALF, 16)
        for d in range(4):
            out_ref[xl4 + d, pl.ds(rows, HALF), :] = part[d * HALF : (d + 1) * HALF]
            for n, stat in enumerate(stats):
                if d % 2:
                    stat = pltpu.roll(
                        jnp.broadcast_to(stat, (8, TILE)), TILE - 64, 1
                    )[:1]
                base = d * HALF - (d % 2) * 64
                for w in range(2):
                    st_scr[xl4 + d, pl.ds(half * 6 + n * 2 + w, 1), :] = stat[
                        :, base + w * 128 : base + (w + 1) * 128
                    ]
        return carry

    lax.fori_loop(0, 4, one_tile, 0)
    for dest in range(TEAM_SIZE):
        out_ref[dest, TOK:, :] = st_scr[dest].astype(jnp.bfloat16)


def project_kernel(got_ref, w0_ref, w1_ref, out_ref, att_scr):
    for half in range(2):
        sides = []
        for w in range(2):
            lse = []
            for k in range(TEAM_SIZE):
                stat = got_ref[k, TOK:, :].astype(jnp.float32)
                row = half * 6 + w
                lse.append(
                    stat[row : row + 1] + stat[row + 2 : row + 3] + stat[row + 4 : row + 5]
                )
            lse = jnp.concatenate(lse, axis=0)
            weight = jnp.exp2(lse - jnp.max(lse, axis=0, keepdims=True))
            weight = weight / jnp.sum(weight, axis=0, keepdims=True)
            sides.append(weight.T)
        weight = jnp.concatenate([sides[0], sides[1][:64]], axis=0)
        total = jnp.zeros((HALF, HD), jnp.float32)
        for k in range(TEAM_SIZE):
            total += weight[:, k : k + 1] * got_ref[
                k, half * HALF : (half + 1) * HALF, :
            ].astype(jnp.float32)
        att_scr[half] = total.astype(jnp.bfloat16)
    own = lax.axis_index("zl") * 2 + lax.axis_index("core")
    out = None
    for w_ref, part, flip in ((w0_ref, 0, 0), (w0_ref, 1, 2), (w1_ref, 0, 1), (w1_ref, 1, 3)):
        rows = pl.multiple_of((own ^ flip) * QUART, 16)
        att = jnp.concatenate(
            [att_scr[half, pl.ds(rows, QUART), :] for half in range(2)], axis=0
        )
        term = jnp.dot(att, w_ref[part], preferred_element_type=jnp.float32)
        out = term if out is None else out + term
    out_ref[...] = out.astype(jnp.bfloat16)


def per_device(queries, keys, values, block_of_slot, doc_lengths, out_weight):
    hbm = pl.BlockSpec(memory_space=pltpu.HBM)
    smem = pl.BlockSpec(memory_space=pltpu.SMEM)
    vmem = pl.BlockSpec(memory_space=pltpu.VMEM)
    spread = pl.pallas_call(
        spread_kernel,
        out_shape=jax.ShapeDtypeStruct((SRC, 4 * QUART, HD), jnp.bfloat16),
        in_specs=[hbm, hbm],
        out_specs=hbm,
        scratch_shapes=[
            pltpu.VMEM((4 * QUART, HD), jnp.bfloat16),
            pltpu.SemaphoreType.DMA((4,)),
            pltpu.SemaphoreType.DMA((SRC,)),
        ],
        name="spread",
    )(keys, values)
    spread, queries, out_weight = lax.optimization_barrier(
        (spread, queries, out_weight)
    )
    kv = lax.all_to_all(spread, KV_AXES, 0, 0, tiled=True)
    flip = [(0, 1), (1, 0)]
    q_side = lax.ppermute(queries, "xl", flip)
    q = lax.all_gather(queries, ("zl", "core"), axis=0, tiled=True)
    q_side = lax.all_gather(q_side, ("zl", "core"), axis=0, tiled=True)
    w_side = lax.ppermute(out_weight, "zl", flip)

    lane = np.arange(TILE)
    in_half = (lane % QUART) // 16 * 64 + lane // HALF * 16 + lane % 16
    i32 = jnp.int32
    rank, in_order, tiles, q_pos, q_start = pl.pallas_call(
        table_kernel,
        out_shape=(
            jax.ShapeDtypeStruct((PIECES + 1,), i32),
            jax.ShapeDtypeStruct((SLOTS,), i32),
            jax.ShapeDtypeStruct((4, 4), i32),
            jax.ShapeDtypeStruct((4, TILE), i32),
            jax.ShapeDtypeStruct((4, TILE), i32),
        ),
        in_specs=[smem, smem, vmem],
        out_specs=(smem, smem, smem, vmem, vmem),
        scratch_shapes=[
            pltpu.SMEM((2 * PIECES,), i32),
            pltpu.SMEM((2 * PIECES + 1,), i32),
        ],
        compiler_params=pltpu.CompilerParams(vmem_limit_bytes=8 << 20),
        name="tables",
    )(block_of_slot, doc_lengths, jnp.asarray(in_half[None, :], i32))

    attend = pl.pallas_call(
        attend_kernel,
        out_shape=jax.ShapeDtypeStruct((TEAM_SIZE, SEND, HD), jnp.bfloat16),
        in_specs=[smem, smem, smem, vmem, vmem, vmem, vmem, vmem],
        out_specs=vmem,
        scratch_shapes=[
            pltpu.VMEM((PAD, HD), jnp.int32),
            pltpu.VMEM((PAD, HD), jnp.bfloat16),
            pltpu.VMEM((PAD, HD), jnp.bfloat16),
            pltpu.VMEM((4, TILE, HD), jnp.bfloat16),
            pltpu.VMEM((1, TILE), jnp.float32),
            pltpu.VMEM((1, TILE), jnp.float32),
            pltpu.VMEM((HD, TILE), jnp.float32),
            pltpu.VMEM((TEAM_SIZE, STAT, HD), jnp.float32),
        ],
        compiler_params=pltpu.CompilerParams(vmem_limit_bytes=16 << 20),
        cost_estimate=pl.CostEstimate(
            flops=4 * 4 * TILE * KEYS * HD,
            transcendentals=4 * TILE * KEYS,
            bytes_accessed=4 << 20,
        ),
        name="attend",
    )
    sent = attend(rank, in_order, tiles, kv, q, q_side, q_pos, q_start)
    _, w_side = lax.optimization_barrier((sent, w_side))
    got = lax.all_to_all(sent, TEAM, 0, 0, tiled=True)
    w0 = jnp.stack([out_weight, w_side])
    w1 = lax.ppermute(w0, "core", flip)
    terms = pl.pallas_call(
        project_kernel,
        out_shape=jax.ShapeDtypeStruct((TOK // 4, out_weight.shape[1]), jnp.bfloat16),
        in_specs=[vmem, vmem, vmem],
        out_specs=vmem,
        scratch_shapes=[pltpu.VMEM((2, HALF, HD), jnp.bfloat16)],
        compiler_params=pltpu.CompilerParams(vmem_limit_bytes=16 << 20),
        name="project",
    )(got, w0, w1)
    parts = lax.all_to_all(terms.reshape(6, 16, -1), Z6, 0, 0, tiled=True)
    return jnp.sum(parts.astype(jnp.float32), axis=0).astype(jnp.bfloat16)


def solution(mesh):
    fine = Mesh(mesh.devices.reshape(SIZES), AXES)
    return jax.shard_map(
        per_device,
        mesh=fine,
        in_specs=(P(DP, HEAD), P(DP, None), P(DP, None), P(), P(), P(HEAD, None)),
        out_specs=P(DP + HEAD, None),
        check_vma=False,
    )
```

```python
import math

import jax
import jax.numpy as jnp
import numpy as np
from jax import lax
from jax.experimental import pallas as pl
from jax.experimental.pallas import tpu as pltpu
from jax.sharding import Mesh, PartitionSpec as P

AXES = ("y", "xh", "xl", "zh", "zm", "zl", "core")
SIZES = (8, 2, 2, 3, 2, 2, 2)
DP = ("y", "xh", "xl")
HEAD = ("zh", "zm", "zl", "core")
TEAM = ("xl", "zl", "core")
KV_GROUPS = [
    [y * 4 + xh * 2 + (kind ^ xh) for y in range(8) for xh in range(2)]
    for kind in range(2)
]
SUM_GROUPS = [
    [p * 4 + (kind ^ p % 2) * 2 + core for p in range(6)]
    for kind in range(2)
    for core in range(2)
]

TOK = 384
HALF = 192
HD = 128
QUART = 48
SRC = 16
PIECES = 2 * SRC
CHUNK = 256
KEYS = PIECES * QUART
PAD = KEYS + CHUNK
SLOTS = PIECES + CHUNK // QUART + 2
TILE = 4 * HALF
LANES = 256
ROWS = 128
TEAM_SIZE = 8
STAT = 16
SEND = TOK + STAT
LOW = -1e30
FAR = 1 << 20
SCALE = math.log2(math.e) / math.sqrt(HD)


def spread_kernel(k_hbm, v_hbm, out_hbm, buf, in_sem, out_sem):
    own = lax.axis_index("zl") * 2 + lax.axis_index("core")
    row = pl.multiple_of(own * QUART, 16)
    col = pl.multiple_of(lax.axis_index("zh") * HD, HD)
    loads = []
    for n, src in enumerate((k_hbm, v_hbm)):
        for half in range(2):
            loads.append(
                pltpu.make_async_copy(
                    src.at[pl.ds(half * HALF + row, QUART), pl.ds(col, HD)],
                    buf.at[pl.ds((2 * n + half) * QUART, QUART), :],
                    in_sem.at[2 * n + half],
                )
            )
    for copy in loads:
        copy.start()
    for copy in loads:
        copy.wait()
    stores = [
        pltpu.make_async_copy(buf, out_hbm.at[n], out_sem.at[n]) for n in range(SRC)
    ]
    for copy in stores:
        copy.start()
    for copy in stores:
        copy.wait()


def start_of(pos, bounds):
    start = jnp.zeros_like(pos)
    for bound in bounds:
        start = jnp.where(pos >= bound, jnp.maximum(start, bound), start)
    return start


def table_kernel(
    slot_ref,
    len_ref,
    lane_ref,
    rank_ref,
    sorted_ref,
    tile_ref,
    qpos_ref,
    qstart_ref,
    where_scr,
    before_scr,
):
    xl = lax.axis_index("xl")
    here = lax.axis_index("y") * 2 + lax.axis_index("xh")
    kind = xl ^ lax.axis_index("xh")

    def clear(n, carry):
        where_scr[n] = PIECES
        return carry

    lax.fori_loop(0, 2 * PIECES, clear, 0)
    for piece in range(PIECES):
        src, half = divmod(piece, 2)
        side = 2 * (kind ^ (src % 2))
        where_scr[slot_ref[4 * src + side + half]] = piece

    def walk(block, count):
        before_scr[block] = count
        piece = where_scr[block]
        rank_ref[piece] = count
        sorted_ref[count] = block
        return count + (piece < PIECES).astype(jnp.int32)

    before_scr[2 * PIECES] = lax.fori_loop(0, 2 * PIECES, walk, jnp.int32(0))
    for n in range(PIECES, SLOTS):
        sorted_ref[n] = FAR // HALF
    bounds = [len_ref[0]]
    for n in range(1, len_ref.shape[0] - 1):
        bounds.append(bounds[-1] + len_ref[n])
    for tile in range(4):
        rel, half = divmod(tile, 2)
        block = slot_ref[4 * here + 2 * (xl ^ rel) + half]
        base = block * HALF
        low = before_scr[lax.div(start_of(base, bounds), HALF)]
        high = before_scr[block + 1]
        tile_ref[tile, 0] = low
        tile_ref[tile, 1] = lax.div((high - low) * QUART + CHUNK - 1, CHUNK)
        tile_ref[tile, 2] = base
        tile_ref[tile, 3] = start_of(base + HALF - 1, bounds)
        pos = lane_ref[pl.ds(lax.axis_index("zm") ^ half, 1), :] + base
        qpos_ref[tile : tile + 1, :] = pos
        qstart_ref[tile : tile + 1, :] = start_of(pos, bounds)


def attend_kernel(
    rank_ref,
    sorted_ref,
    tile_ref,
    kv_ref,
    q_own_ref,
    q_side_ref,
    qpos_ref,
    qstart_ref,
    out_ref,
    kpos_scr,
    k_scr,
    v_scr,
    q_scr,
    m_scr,
    l_scr,
    acc_scr,
    st_scr,
):
    for piece in range(PIECES):
        src, half = divmod(piece, 2)
        at = pl.multiple_of(rank_ref[piece] * QUART, 16)
        k_scr[pl.ds(at, QUART), :] = kv_ref[src, half * QUART : (half + 1) * QUART, :]
        v_scr[pl.ds(at, QUART), :] = kv_ref[
            src, (2 + half) * QUART : (3 + half) * QUART, :
        ]
    k_scr[KEYS:, :] = jnp.zeros((CHUNK, HD), jnp.bfloat16)
    v_scr[KEYS:, :] = jnp.zeros((CHUNK, HD), jnp.bfloat16)
    st_scr[...] = jnp.zeros_like(st_scr)
    own = lax.axis_index("zl") * 2 + lax.axis_index("core")
    row = lax.broadcasted_iota(jnp.int32, (QUART, HD), 0) + own * QUART
    for n in range(PIECES):
        kpos_scr[n * QUART : (n + 1) * QUART, :] = row + sorted_ref[n] * HALF
    kpos_scr[KEYS:, :] = jnp.full((PAD - KEYS, HD), FAR, jnp.int32)

    zm = lax.axis_index("zm")
    flips = (zm * 32, (1 - zm) * 32)
    for tile in range(4):
        q_ref = (q_own_ref, q_side_ref)[tile // 2]
        half = tile % 2
        for d in range(4):
            for j in range(4):
                for z3 in range(3):
                    to = d * HALF + j * QUART + z3 * 16
                    of = j * TOK + half * HALF + z3 * 64
                    of = of + ((d * 16) ^ flips[(half * 3 + z3) % 2])
                    rows = pl.ds(pl.multiple_of(of, 16), 16)
                    q_scr[tile, to : to + 16, :] = q_ref[rows, :]

    def one_tile(tile, carry):
        low, steps, q_first, start_last = (tile_ref[tile, n] for n in range(4))
        m_scr[...] = jnp.full_like(m_scr, LOW)
        l_scr[...] = jnp.zeros_like(l_scr)
        acc_scr[...] = jnp.zeros_like(acc_scr)

        def one_step(step, carry):
            first = low * QUART + step * CHUNK
            at = pl.multiple_of(first, 16)
            first_pos = sorted_ref[lax.div(first, QUART)] * HALF
            last_pos = sorted_ref[lax.div(first + CHUNK - 1, QUART)] * HALF + HALF - 1
            edge = (last_pos > q_first) | (first_pos < start_last)

            def block(masked):
                parts = TILE // LANES
                keys = [
                    k_scr[pl.ds(at + r * ROWS, ROWS), :] for r in range(CHUNK // ROWS)
                ]
                vals = v_scr[pl.ds(at, CHUNK), :]

                def score(part, r):
                    cols = slice(part * LANES, (part + 1) * LANES)
                    scores = lax.dot_general(
                        keys[r],
                        q_scr[tile, cols, :],
                        (((1,), (1,)), ((), ())),
                        preferred_element_type=jnp.float32,
                    )
                    if masked:
                        key_pos = kpos_scr[pl.ds(at + r * ROWS, ROWS), :]
                        key_pos = jnp.concatenate([key_pos] * (LANES // HD), axis=1)
                        allowed = (key_pos <= qpos_ref[pl.ds(tile, 1), cols]) & (
                            key_pos >= qstart_ref[pl.ds(tile, 1), cols]
                        )
                        scores = jnp.where(allowed, scores, LOW)
                    return scores

                ahead = [score(0, r) for r in range(CHUNK // ROWS)]
                for part in range(parts):
                    cols = slice(part * LANES, (part + 1) * LANES)
                    now, ahead = ahead, []
                    high = now[0]
                    for scores in now[1:]:
                        high = jnp.maximum(high, scores)
                    old = m_scr[:, cols]
                    new = jnp.maximum(old, jnp.max(high, axis=0, keepdims=True))
                    m_scr[:, cols] = new
                    factor = jnp.exp2((old - new) * SCALE)
                    probs, total = [], None
                    for r, scores in enumerate(now):
                        if part + 1 < parts:
                            ahead.append(score(part + 1, r))
                        prob = jnp.exp2((scores - new) * SCALE)
                        total = prob if total is None else total + prob
                        probs.append(prob.astype(jnp.bfloat16))
                    l_scr[:, cols] = l_scr[:, cols] * factor + jnp.sum(
                        total, axis=0, keepdims=True
                    )
                    acc_scr[:, cols] = acc_scr[:, cols] * factor + lax.dot_general(
                        vals,
                        jnp.concatenate(probs, axis=0),
                        (((0,), (0,)), ((), ())),
                        preferred_element_type=jnp.float32,
                    )

            pl.when(edge)(lambda: block(True))
            pl.when(jnp.logical_not(edge))(lambda: block(False))
            return carry

        lax.fori_loop(0, steps, one_step, 0)
        total = jnp.where(l_scr[...] > 0, l_scr[...], 1.0)
        part = (acc_scr[...] / total).T.astype(jnp.bfloat16)
        lse = m_scr[...] * SCALE + jnp.log2(total)
        high = lse.astype(jnp.bfloat16).astype(jnp.float32)
        mid = (lse - high).astype(jnp.bfloat16).astype(jnp.float32)
        stats = (high, mid, lse - high - mid)
        xl4 = ((tile >> 1) ^ lax.axis_index("xl")) * 4
        half = tile & 1
        rows = pl.multiple_of(half * HALF, 16)
        for d in range(4):
            out_ref[xl4 + d, pl.ds(rows, HALF), :] = part[d * HALF : (d + 1) * HALF]
            for n, stat in enumerate(stats):
                if d % 2:
                    stat = pltpu.roll(
                        jnp.broadcast_to(stat, (8, TILE)), TILE - 64, 1
                    )[:1]
                base = d * HALF - (d % 2) * 64
                for w in range(2):
                    st_scr[xl4 + d, pl.ds(half * 6 + n * 2 + w, 1), :] = stat[
                        :, base + w * 128 : base + (w + 1) * 128
                    ]
        return carry

    lax.fori_loop(0, 4, one_tile, 0)
    for dest in range(TEAM_SIZE):
        out_ref[dest, TOK:, :] = st_scr[dest].astype(jnp.bfloat16)


def project_kernel(got_ref, w0_ref, w1_ref, out_ref, att_scr):
    for half in range(2):
        sides = []
        for w in range(2):
            lse = []
            for k in range(TEAM_SIZE):
                stat = got_ref[k, TOK:, :].astype(jnp.float32)
                row = half * 6 + w
                lse.append(
                    stat[row : row + 1] + stat[row + 2 : row + 3] + stat[row + 4 : row + 5]
                )
            lse = jnp.concatenate(lse, axis=0)
            weight = jnp.exp2(lse - jnp.max(lse, axis=0, keepdims=True))
            weight = weight / jnp.sum(weight, axis=0, keepdims=True)
            sides.append(weight.T)
        weight = jnp.concatenate([sides[0], sides[1][:64]], axis=0)
        total = jnp.zeros((HALF, HD), jnp.float32)
        for k in range(TEAM_SIZE):
            total += weight[:, k : k + 1] * got_ref[
                k, half * HALF : (half + 1) * HALF, :
            ].astype(jnp.float32)
        att_scr[half] = total.astype(jnp.bfloat16)
    own = lax.axis_index("zl") * 2 + lax.axis_index("core")
    out = None
    for w_ref, part, flip in ((w0_ref, 0, 0), (w0_ref, 1, 2), (w1_ref, 0, 1), (w1_ref, 1, 3)):
        rows = pl.multiple_of((own ^ flip) * QUART, 16)
        att = jnp.concatenate(
            [att_scr[half, pl.ds(rows, QUART), :] for half in range(2)], axis=0
        )
        term = jnp.dot(att, w_ref[part], preferred_element_type=jnp.float32)
        out = term if out is None else out + term
    out_ref[...] = out.astype(jnp.bfloat16)


def per_device(queries, keys, values, block_of_slot, doc_lengths, out_weight):
    hbm = pl.BlockSpec(memory_space=pltpu.HBM)
    smem = pl.BlockSpec(memory_space=pltpu.SMEM)
    vmem = pl.BlockSpec(memory_space=pltpu.VMEM)
    spread = pl.pallas_call(
        spread_kernel,
        out_shape=jax.ShapeDtypeStruct((SRC, 4 * QUART, HD), jnp.bfloat16),
        in_specs=[hbm, hbm],
        out_specs=hbm,
        scratch_shapes=[
            pltpu.VMEM((4 * QUART, HD), jnp.bfloat16),
            pltpu.SemaphoreType.DMA((4,)),
            pltpu.SemaphoreType.DMA((SRC,)),
        ],
        name="spread",
    )(keys, values)
    spread, queries, out_weight = lax.optimization_barrier(
        (spread, queries, out_weight)
    )
    kv = lax.all_to_all(
        spread, DP, 0, 0, axis_index_groups=KV_GROUPS, tiled=True
    )
    flip = [(0, 1), (1, 0)]
    q_side = lax.ppermute(queries, "xl", flip)
    q = lax.all_gather(queries, ("zl", "core"), axis=0, tiled=True)
    q_side = lax.all_gather(q_side, ("zl", "core"), axis=0, tiled=True)
    w_side = lax.ppermute(out_weight, "zl", flip)

    lane = np.arange(TILE)
    third = lane % QUART // 16
    in_half = np.stack(
        [
            third * 64 + (lane // HALF * 16 ^ (n ^ third % 2) * 32) + lane % 16
            for n in range(2)
        ]
    )
    i32 = jnp.int32
    rank, in_order, tiles, q_pos, q_start = pl.pallas_call(
        table_kernel,
        out_shape=(
            jax.ShapeDtypeStruct((PIECES + 1,), i32),
            jax.ShapeDtypeStruct((SLOTS,), i32),
            jax.ShapeDtypeStruct((4, 4), i32),
            jax.ShapeDtypeStruct((4, TILE), i32),
            jax.ShapeDtypeStruct((4, TILE), i32),
        ),
        in_specs=[smem, smem, vmem],
        out_specs=(smem, smem, smem, vmem, vmem),
        scratch_shapes=[
            pltpu.SMEM((2 * PIECES,), i32),
            pltpu.SMEM((2 * PIECES + 1,), i32),
        ],
        compiler_params=pltpu.CompilerParams(vmem_limit_bytes=8 << 20),
        name="tables",
    )(block_of_slot, doc_lengths, jnp.asarray(in_half, i32))

    attend = pl.pallas_call(
        attend_kernel,
        out_shape=jax.ShapeDtypeStruct((TEAM_SIZE, SEND, HD), jnp.bfloat16),
        in_specs=[smem, smem, smem, vmem, vmem, vmem, vmem, vmem],
        out_specs=vmem,
        scratch_shapes=[
            pltpu.VMEM((PAD, HD), jnp.int32),
            pltpu.VMEM((PAD, HD), jnp.bfloat16),
            pltpu.VMEM((PAD, HD), jnp.bfloat16),
            pltpu.VMEM((4, TILE, HD), jnp.bfloat16),
            pltpu.VMEM((1, TILE), jnp.float32),
            pltpu.VMEM((1, TILE), jnp.float32),
            pltpu.VMEM((HD, TILE), jnp.float32),
            pltpu.VMEM((TEAM_SIZE, STAT, HD), jnp.float32),
        ],
        compiler_params=pltpu.CompilerParams(vmem_limit_bytes=16 << 20),
        cost_estimate=pl.CostEstimate(
            flops=4 * 4 * TILE * KEYS * HD,
            transcendentals=4 * TILE * KEYS,
            bytes_accessed=4 << 20,
        ),
        name="attend",
    )
    sent = attend(rank, in_order, tiles, kv, q, q_side, q_pos, q_start)
    _, w_side = lax.optimization_barrier((sent, w_side))
    got = lax.all_to_all(sent, TEAM, 0, 0, tiled=True)
    w0 = jnp.stack([out_weight, w_side])
    w1 = lax.ppermute(w0, "core", flip)
    terms = pl.pallas_call(
        project_kernel,
        out_shape=jax.ShapeDtypeStruct((TOK // 4, out_weight.shape[1]), jnp.bfloat16),
        in_specs=[vmem, vmem, vmem],
        out_specs=vmem,
        scratch_shapes=[pltpu.VMEM((2, HALF, HD), jnp.bfloat16)],
        compiler_params=pltpu.CompilerParams(vmem_limit_bytes=16 << 20),
        name="project",
    )(got, w0, w1)
    parts = lax.all_to_all(
        terms.reshape(6, 16, -1), HEAD, 0, 0, axis_index_groups=SUM_GROUPS, tiled=True
    )
    return jnp.sum(parts.astype(jnp.float32), axis=0).astype(jnp.bfloat16)


def solution(mesh):
    fine = Mesh(mesh.devices.reshape(SIZES), AXES)
    return jax.shard_map(
        per_device,
        mesh=fine,
        in_specs=(P(DP, HEAD), P(DP, None), P(DP, None), P(), P(), P(HEAD, None)),
        out_specs=P(DP + HEAD, None),
        check_vma=False,
    )
```

```python
import math

import jax
import jax.numpy as jnp
import numpy as np
from jax import lax
from jax.experimental import pallas as pl
from jax.experimental.pallas import tpu as pltpu
from jax.sharding import Mesh, PartitionSpec as P

AXES = ("y", "xh", "xl", "zh", "zm", "zl", "core")
SIZES = (8, 2, 2, 3, 2, 2, 2)
DP = ("y", "xh", "xl")
HEAD = ("zh", "zm", "zl", "core")
TEAM = ("xl", "zl", "core")
KV_GROUPS = [
    [y * 4 + xh * 2 + (kind ^ xh) for y in range(8) for xh in range(2)]
    for kind in range(2)
]
Z6 = ("zh", "zm")

TOK = 384
HALF = 192
HD = 128
QUART = 48
SRC = 16
PIECES = 2 * SRC
CHUNK = 256
KEYS = PIECES * QUART
PAD = KEYS + CHUNK
SLOTS = PIECES + CHUNK // QUART + 2
TILE = 4 * HALF
LANES = 256
ROWS = 128
GROUPS = CHUNK // ROWS
TEAM_SIZE = 8
STAT = 16
SEND = TOK + STAT
LOW = -1e30
FAR = 1 << 20
SCALE = math.log2(math.e) / math.sqrt(HD)


def spread_kernel(k_hbm, v_hbm, out_hbm, buf, in_sem, out_sem):
    own = lax.axis_index("zl") * 2 + lax.axis_index("core")
    row = pl.multiple_of(own * QUART, 16)
    col = pl.multiple_of(lax.axis_index("zh") * HD, HD)
    loads = []
    for n, src in enumerate((k_hbm, v_hbm)):
        for half in range(2):
            loads.append(
                pltpu.make_async_copy(
                    src.at[pl.ds(half * HALF + row, QUART), pl.ds(col, HD)],
                    buf.at[pl.ds((2 * n + half) * QUART, QUART), :],
                    in_sem.at[2 * n + half],
                )
            )
    for copy in loads:
        copy.start()
    for copy in loads:
        copy.wait()
    stores = [
        pltpu.make_async_copy(buf, out_hbm.at[n], out_sem.at[n]) for n in range(SRC)
    ]
    for copy in stores:
        copy.start()
    for copy in stores:
        copy.wait()


def start_of(pos, bounds):
    start = jnp.zeros_like(pos)
    for bound in bounds:
        start = jnp.where(pos >= bound, jnp.maximum(start, bound), start)
    return start


def table_kernel(
    slot_ref,
    len_ref,
    lane_ref,
    rank_ref,
    sorted_ref,
    tile_ref,
    qpos_ref,
    qstart_ref,
    where_scr,
    before_scr,
):
    xl = lax.axis_index("xl")
    here = lax.axis_index("y") * 2 + lax.axis_index("xh")
    kind = xl ^ lax.axis_index("xh")

    def clear(n, carry):
        where_scr[n] = PIECES
        return carry

    lax.fori_loop(0, 2 * PIECES, clear, 0)
    for piece in range(PIECES):
        src, half = divmod(piece, 2)
        side = 2 * (kind ^ (src % 2))
        where_scr[slot_ref[4 * src + side + half]] = piece

    def walk(block, count):
        before_scr[block] = count
        piece = where_scr[block]
        rank_ref[piece] = count
        sorted_ref[count] = block
        return count + (piece < PIECES).astype(jnp.int32)

    before_scr[2 * PIECES] = lax.fori_loop(0, 2 * PIECES, walk, jnp.int32(0))
    for n in range(PIECES, SLOTS):
        sorted_ref[n] = FAR // HALF
    bounds = [len_ref[0]]
    for n in range(1, len_ref.shape[0] - 1):
        bounds.append(bounds[-1] + len_ref[n])
    for tile in range(4):
        rel, half = divmod(tile, 2)
        block = slot_ref[4 * here + 2 * (xl ^ rel) + half]
        base = block * HALF
        low = before_scr[lax.div(start_of(base, bounds), HALF)]
        high = before_scr[block + 1]
        tile_ref[tile, 0] = low
        tile_ref[tile, 1] = lax.div((high - low) * QUART + CHUNK - 1, CHUNK)
        tile_ref[tile, 2] = base
        tile_ref[tile, 3] = start_of(base + HALF - 1, bounds)
        pos = lane_ref[...] + base
        qpos_ref[tile : tile + 1, :] = pos
        qstart_ref[tile : tile + 1, :] = start_of(pos, bounds)


def attend_kernel(
    rank_ref,
    sorted_ref,
    tile_ref,
    kv_ref,
    q_own_ref,
    q_side_ref,
    qpos_ref,
    qstart_ref,
    out_ref,
    kpos_scr,
    k_scr,
    v_scr,
    q_scr,
    s_scr,
    m_scr,
    l_scr,
    acc_scr,
    st_scr,
):
    for piece in range(PIECES):
        src, half = divmod(piece, 2)
        at = pl.multiple_of(rank_ref[piece] * QUART, 16)
        k_scr[pl.ds(at, QUART), :] = kv_ref[src, half * QUART : (half + 1) * QUART, :]
        v_scr[pl.ds(at, QUART), :] = kv_ref[
            src, (2 + half) * QUART : (3 + half) * QUART, :
        ]
    k_scr[KEYS:, :] = jnp.zeros((CHUNK, HD), jnp.bfloat16)
    v_scr[KEYS:, :] = jnp.zeros((CHUNK, HD), jnp.bfloat16)
    st_scr[...] = jnp.zeros_like(st_scr)
    own = lax.axis_index("zl") * 2 + lax.axis_index("core")
    row = lax.broadcasted_iota(jnp.int32, (QUART, HD), 0) + own * QUART
    for n in range(PIECES):
        kpos_scr[n * QUART : (n + 1) * QUART, :] = row + sorted_ref[n] * HALF
    kpos_scr[KEYS:, :] = jnp.full((PAD - KEYS, HD), FAR, jnp.int32)

    for tile in range(4):
        q_ref = (q_own_ref, q_side_ref)[tile // 2]
        half = tile % 2
        for d in range(4):
            for j in range(4):
                for z3 in range(3):
                    to = d * HALF + j * QUART + z3 * 16
                    of = j * TOK + half * HALF + z3 * 64 + d * 16
                    q_scr[tile, to : to + 16, :] = q_ref[of : of + 16, :]

    def score(tile, at, part, r):
        return lax.dot_general(
            k_scr[pl.ds(at + r * ROWS, ROWS), :],
            q_scr[tile, part * LANES : (part + 1) * LANES, :],
            (((1,), (1,)), ((), ())),
            preferred_element_type=jnp.float32,
        )

    def one_tile(tile, carry):
        low, steps, q_first, start_last = (tile_ref[tile, n] for n in range(4))
        m_scr[...] = jnp.full_like(m_scr, LOW)
        l_scr[...] = jnp.zeros_like(l_scr)
        acc_scr[...] = jnp.zeros_like(acc_scr)

        start = pl.multiple_of(low * QUART, 16)
        for r in range(GROUPS):
            s_scr[r * ROWS : (r + 1) * ROWS, :] = score(tile, start, 0, r)

        def one_step(step, carry):
            first = low * QUART + step * CHUNK
            at = pl.multiple_of(first, 16)
            first_pos = sorted_ref[lax.div(first, QUART)] * HALF
            last_pos = sorted_ref[lax.div(first + CHUNK - 1, QUART)] * HALF + HALF - 1
            edge = (last_pos > q_first) | (first_pos < start_last)

            after = pl.multiple_of(jnp.minimum(first + CHUNK, KEYS), 16)

            def block(masked):
                parts = TILE // LANES
                vals = v_scr[pl.ds(at, CHUNK), :]
                waiting = []

                def collect():
                    cols, factor, probs = waiting.pop(0)
                    acc_scr[:, cols] = acc_scr[:, cols] * factor + lax.dot_general(
                        vals,
                        probs,
                        (((0,), (0,)), ((), ())),
                        preferred_element_type=jnp.float32,
                    )

                ahead = [s_scr[r * ROWS : (r + 1) * ROWS, :] for r in range(GROUPS)]
                for part in range(parts):
                    cols = slice(part * LANES, (part + 1) * LANES)
                    now, ahead = ahead, []
                    if masked:
                        for r in range(GROUPS):
                            key_pos = kpos_scr[pl.ds(at + r * ROWS, ROWS), :]
                            key_pos = jnp.concatenate([key_pos] * (LANES // HD), axis=1)
                            allowed = (key_pos <= qpos_ref[pl.ds(tile, 1), cols]) & (
                                key_pos >= qstart_ref[pl.ds(tile, 1), cols]
                            )
                            now[r] = jnp.where(allowed, now[r], LOW)
                    high = now[0]
                    for scores in now[1:]:
                        high = jnp.maximum(high, scores)
                    old = m_scr[:, cols]
                    new = jnp.maximum(old, jnp.max(high, axis=0, keepdims=True))
                    m_scr[:, cols] = new
                    factor = jnp.exp2((old - new) * SCALE)
                    probs, total = [], None
                    for r, scores in enumerate(now):
                        if part + 1 < parts:
                            ahead.append(score(tile, at, part + 1, r))
                        else:
                            ahead.append(score(tile, after, 0, r))
                        prob = jnp.exp2((scores - new) * SCALE)
                        total = prob if total is None else total + prob
                        probs.append(prob.astype(jnp.bfloat16))
                    l_scr[:, cols] = l_scr[:, cols] * factor + jnp.sum(
                        total, axis=0, keepdims=True
                    )
                    waiting.append((cols, factor, jnp.concatenate(probs, axis=0)))
                    if part:
                        collect()
                collect()
                for r in range(GROUPS):
                    s_scr[r * ROWS : (r + 1) * ROWS, :] = ahead[r]

            pl.when(edge)(lambda: block(True))
            pl.when(jnp.logical_not(edge))(lambda: block(False))
            return carry

        lax.fori_loop(0, steps, one_step, 0)
        total = jnp.where(l_scr[...] > 0, l_scr[...], 1.0)
        part = (acc_scr[...] / total).T.astype(jnp.bfloat16)
        lse = m_scr[...] * SCALE + jnp.log2(total)
        high = lse.astype(jnp.bfloat16).astype(jnp.float32)
        mid = (lse - high).astype(jnp.bfloat16).astype(jnp.float32)
        stats = (high, mid, lse - high - mid)
        xl4 = ((tile >> 1) ^ lax.axis_index("xl")) * 4
        half = tile & 1
        rows = pl.multiple_of(half * HALF, 16)
        for d in range(4):
            out_ref[xl4 + d, pl.ds(rows, HALF), :] = part[d * HALF : (d + 1) * HALF]
            for n, stat in enumerate(stats):
                if d % 2:
                    stat = pltpu.roll(
                        jnp.broadcast_to(stat, (8, TILE)), TILE - 64, 1
                    )[:1]
                base = d * HALF - (d % 2) * 64
                for w in range(2):
                    st_scr[xl4 + d, pl.ds(half * 6 + n * 2 + w, 1), :] = stat[
                        :, base + w * 128 : base + (w + 1) * 128
                    ]
        return carry

    lax.fori_loop(0, 4, one_tile, 0)
    for dest in range(TEAM_SIZE):
        out_ref[dest, TOK:, :] = st_scr[dest].astype(jnp.bfloat16)


def project_kernel(got_ref, w0_ref, w1_ref, out_ref, att_scr):
    for half in range(2):
        sides = []
        for w in range(2):
            lse = []
            for k in range(TEAM_SIZE):
                stat = got_ref[k, TOK:, :].astype(jnp.float32)
                row = half * 6 + w
                lse.append(
                    stat[row : row + 1] + stat[row + 2 : row + 3] + stat[row + 4 : row + 5]
                )
            lse = jnp.concatenate(lse, axis=0)
            weight = jnp.exp2(lse - jnp.max(lse, axis=0, keepdims=True))
            weight = weight / jnp.sum(weight, axis=0, keepdims=True)
            sides.append(weight.T)
        weight = jnp.concatenate([sides[0], sides[1][:64]], axis=0)
        total = jnp.zeros((HALF, HD), jnp.float32)
        for k in range(TEAM_SIZE):
            total += weight[:, k : k + 1] * got_ref[
                k, half * HALF : (half + 1) * HALF, :
            ].astype(jnp.float32)
        att_scr[half] = total.astype(jnp.bfloat16)
    own = lax.axis_index("zl") * 2 + lax.axis_index("core")
    out = None
    for w_ref, part, flip in ((w0_ref, 0, 0), (w0_ref, 1, 2), (w1_ref, 0, 1), (w1_ref, 1, 3)):
        rows = pl.multiple_of((own ^ flip) * QUART, 16)
        att = jnp.concatenate(
            [att_scr[half, pl.ds(rows, QUART), :] for half in range(2)], axis=0
        )
        term = jnp.dot(att, w_ref[part], preferred_element_type=jnp.float32)
        out = term if out is None else out + term
    out_ref[...] = out.astype(jnp.bfloat16)


def per_device(queries, keys, values, block_of_slot, doc_lengths, out_weight):
    hbm = pl.BlockSpec(memory_space=pltpu.HBM)
    smem = pl.BlockSpec(memory_space=pltpu.SMEM)
    vmem = pl.BlockSpec(memory_space=pltpu.VMEM)
    spread = pl.pallas_call(
        spread_kernel,
        out_shape=jax.ShapeDtypeStruct((SRC, 4 * QUART, HD), jnp.bfloat16),
        in_specs=[hbm, hbm],
        out_specs=hbm,
        scratch_shapes=[
            pltpu.VMEM((4 * QUART, HD), jnp.bfloat16),
            pltpu.SemaphoreType.DMA((4,)),
            pltpu.SemaphoreType.DMA((SRC,)),
        ],
        name="spread",
    )(keys, values)
    spread, queries, out_weight = lax.optimization_barrier(
        (spread, queries, out_weight)
    )
    kv = lax.all_to_all(
        spread, DP, 0, 0, axis_index_groups=KV_GROUPS, tiled=True
    )
    flip = [(0, 1), (1, 0)]
    q_side = lax.ppermute(queries, "xl", flip)
    q = lax.all_gather(queries, ("zl", "core"), axis=0, tiled=True)
    q_side = lax.all_gather(q_side, ("zl", "core"), axis=0, tiled=True)
    w_side = lax.ppermute(out_weight, "zl", flip)

    lane = np.arange(TILE)
    in_half = lane % QUART // 16 * 64 + lane // HALF * 16 + lane % 16
    i32 = jnp.int32
    rank, in_order, tiles, q_pos, q_start = pl.pallas_call(
        table_kernel,
        out_shape=(
            jax.ShapeDtypeStruct((PIECES + 1,), i32),
            jax.ShapeDtypeStruct((SLOTS,), i32),
            jax.ShapeDtypeStruct((4, 4), i32),
            jax.ShapeDtypeStruct((4, TILE), i32),
            jax.ShapeDtypeStruct((4, TILE), i32),
        ),
        in_specs=[smem, smem, vmem],
        out_specs=(smem, smem, smem, vmem, vmem),
        scratch_shapes=[
            pltpu.SMEM((2 * PIECES,), i32),
            pltpu.SMEM((2 * PIECES + 1,), i32),
        ],
        compiler_params=pltpu.CompilerParams(vmem_limit_bytes=8 << 20),
        name="tables",
    )(block_of_slot, doc_lengths, jnp.asarray(in_half[None, :], i32))

    attend = pl.pallas_call(
        attend_kernel,
        out_shape=jax.ShapeDtypeStruct((TEAM_SIZE, SEND, HD), jnp.bfloat16),
        in_specs=[smem, smem, smem, vmem, vmem, vmem, vmem, vmem],
        out_specs=vmem,
        scratch_shapes=[
            pltpu.VMEM((PAD, HD), jnp.int32),
            pltpu.VMEM((PAD, HD), jnp.bfloat16),
            pltpu.VMEM((PAD, HD), jnp.bfloat16),
            pltpu.VMEM((4, TILE, HD), jnp.bfloat16),
            pltpu.VMEM((CHUNK, LANES), jnp.float32),
            pltpu.VMEM((1, TILE), jnp.float32),
            pltpu.VMEM((1, TILE), jnp.float32),
            pltpu.VMEM((HD, TILE), jnp.float32),
            pltpu.VMEM((TEAM_SIZE, STAT, HD), jnp.float32),
        ],
        compiler_params=pltpu.CompilerParams(vmem_limit_bytes=16 << 20),
        cost_estimate=pl.CostEstimate(
            flops=4 * 4 * TILE * KEYS * HD,
            transcendentals=4 * TILE * KEYS,
            bytes_accessed=4 << 20,
        ),
        name="attend",
    )
    sent = attend(rank, in_order, tiles, kv, q, q_side, q_pos, q_start)
    _, w_side = lax.optimization_barrier((sent, w_side))
    got = lax.all_to_all(sent, TEAM, 0, 0, tiled=True)
    w0 = jnp.stack([out_weight, w_side])
    w1 = lax.ppermute(w0, "core", flip)
    terms = pl.pallas_call(
        project_kernel,
        out_shape=jax.ShapeDtypeStruct((TOK // 4, out_weight.shape[1]), jnp.bfloat16),
        in_specs=[vmem, vmem, vmem],
        out_specs=vmem,
        scratch_shapes=[pltpu.VMEM((2, HALF, HD), jnp.bfloat16)],
        compiler_params=pltpu.CompilerParams(vmem_limit_bytes=16 << 20),
        name="project",
    )(got, w0, w1)
    parts = lax.all_to_all(
        terms.reshape(6, 16, -1), Z6, 0, 0, tiled=True
    )
    return jnp.sum(parts.astype(jnp.float32), axis=0).astype(jnp.bfloat16)


def solution(mesh):
    fine = Mesh(mesh.devices.reshape(SIZES), AXES)
    return jax.shard_map(
        per_device,
        mesh=fine,
        in_specs=(P(DP, HEAD), P(DP, None), P(DP, None), P(), P(), P(HEAD, None)),
        out_specs=P(DP + HEAD, None),
        check_vma=False,
    )
```

```python
import math

import jax
import jax.numpy as jnp
import numpy as np
from jax import lax
from jax.experimental import pallas as pl
from jax.experimental.pallas import tpu as pltpu
from jax.sharding import Mesh, PartitionSpec as P

AXES = ("y", "xh", "xl", "zh", "zm", "zl", "core")
SIZES = (8, 2, 2, 3, 2, 2, 2)
DP = ("y", "xh", "xl")
HEAD = ("zh", "zm", "zl", "core")
TEAM = ("xl", "zl", "core")
Z6 = ("zh", "zm")

TOK = 384
HALF = 192
HD = 128
QUART = 48
KROWS = 24
SRC = 32
PIECES = 2 * SRC
CHUNK = 256
KEYS = PIECES * KROWS
PAD = KEYS + CHUNK
TILE = 4 * HALF
LANES = 256
ROWS = 128
GROUPS = CHUNK // ROWS
TEAM_SIZE = 8
STAT = 16
SEND = TOK + STAT
LOW = -1e30
FAR = 1 << 20
SCALE = math.log2(math.e) / math.sqrt(HD)


def team_index():
    own = lax.axis_index("zl") * 2 + lax.axis_index("core")
    return lax.axis_index("xl") * 4 + own


def spread_kernel(k_hbm, v_hbm, out_hbm, buf, in_sem, out_sem):
    own = lax.axis_index("zl") * 2 + lax.axis_index("core")
    col = pl.multiple_of(lax.axis_index("zh") * HD, HD)
    loads = []
    for side in range(2):
        row = pl.multiple_of((side * 4 + own) * KROWS, 8)
        for n, src in enumerate((k_hbm, v_hbm)):
            for half in range(2):
                loads.append(
                    pltpu.make_async_copy(
                        src.at[pl.ds(half * HALF + row, KROWS), pl.ds(col, HD)],
                        buf.at[side, pl.ds((2 * n + half) * KROWS, KROWS), :],
                        in_sem.at[4 * side + 2 * n + half],
                    )
                )
    for copy in loads:
        copy.start()
    for copy in loads:
        copy.wait()
    stores = [
        pltpu.make_async_copy(buf.at[n % 2], out_hbm.at[n], out_sem.at[n]) for n in range(SRC)
    ]
    for copy in stores:
        copy.start()
    for copy in stores:
        copy.wait()


def start_of(pos, bounds):
    start = jnp.zeros_like(pos)
    for bound in bounds:
        start = jnp.where(pos >= bound, jnp.maximum(start, bound), start)
    return start


def table_kernel(slot_ref, len_ref, lane_ref, tile_ref, qpos_ref, qstart_ref):
    here = lax.axis_index("y") * 2 + lax.axis_index("xh")
    bounds = [len_ref[0]]
    for n in range(1, len_ref.shape[0] - 1):
        bounds.append(bounds[-1] + len_ref[n])
    for tile in range(4):
        rel, half = divmod(tile, 2)
        block = slot_ref[4 * here + 2 * (lax.axis_index("xl") ^ rel) + half]
        base = block * HALF
        low = lax.div(start_of(base, bounds), HALF)
        tile_ref[tile, 0] = low
        tile_ref[tile, 1] = lax.div((block + 1 - low) * KROWS + CHUNK - 1, CHUNK)
        tile_ref[tile, 2] = base
        tile_ref[tile, 3] = start_of(base + HALF - 1, bounds)
        pos = lane_ref[...] + base
        qpos_ref[tile : tile + 1, :] = pos
        qstart_ref[tile : tile + 1, :] = start_of(pos, bounds)


def attend_kernel(
    slot_ref,
    tile_ref,
    kv_ref,
    q_own_ref,
    q_side_ref,
    qpos_ref,
    qstart_ref,
    out_ref,
    kpos_scr,
    k_scr,
    v_scr,
    q_scr,
    s_scr,
    m_scr,
    l_scr,
    acc_scr,
    st_scr,
):
    for piece in range(PIECES):
        src, half = divmod(piece, 2)
        at = pl.multiple_of(slot_ref[piece] * KROWS, 8)
        for n, scr in enumerate((k_scr, v_scr)):
            rows = slice((2 * n + half) * KROWS, (2 * n + half + 1) * KROWS)
            scr[pl.ds(at, KROWS), :] = kv_ref[src, rows, :].astype(jnp.float32)
    k_scr[KEYS:, :] = jnp.zeros((CHUNK, HD), jnp.float32)
    v_scr[KEYS:, :] = jnp.zeros((CHUNK, HD), jnp.float32)
    st_scr[...] = jnp.zeros_like(st_scr)
    row = lax.broadcasted_iota(jnp.int32, (KROWS, HD), 0) + team_index() * KROWS
    for n in range(PIECES):
        kpos_scr[n * KROWS : (n + 1) * KROWS, :] = row + n * HALF
    kpos_scr[KEYS:, :] = jnp.full((PAD - KEYS, HD), FAR, jnp.int32)

    for tile in range(4):
        q_ref = (q_own_ref, q_side_ref)[tile // 2]
        half = tile % 2
        for d in range(4):
            for j in range(4):
                for z3 in range(3):
                    to = d * HALF + j * QUART + z3 * 16
                    of = j * TOK + half * HALF + z3 * 64 + d * 16
                    q_scr[tile, to : to + 16, :] = q_ref[of : of + 16, :]

    def score(tile, at, part, r):
        return lax.dot_general(
            k_scr[pl.ds(at + r * ROWS, ROWS), :].astype(jnp.bfloat16),
            q_scr[tile, part * LANES : (part + 1) * LANES, :],
            (((1,), (1,)), ((), ())),
            preferred_element_type=jnp.float32,
        )

    def one_tile(tile, carry):
        low, steps, q_first, start_last = (tile_ref[tile, n] for n in range(4))
        m_scr[...] = jnp.full_like(m_scr, LOW)
        l_scr[...] = jnp.zeros_like(l_scr)
        acc_scr[...] = jnp.zeros_like(acc_scr)

        start = pl.multiple_of(low * KROWS, 8)
        for r in range(GROUPS):
            s_scr[r * ROWS : (r + 1) * ROWS, :] = score(tile, start, 0, r)

        def one_step(step, carry):
            first = low * KROWS + step * CHUNK
            at = pl.multiple_of(first, 8)
            first_pos = lax.div(first, KROWS) * HALF
            last_pos = lax.div(first + CHUNK - 1, KROWS) * HALF + HALF - 1
            edge = (last_pos > q_first) | (first_pos < start_last)

            after = pl.multiple_of(jnp.minimum(first + CHUNK, KEYS), 8)

            def block(masked):
                parts = TILE // LANES
                vals = v_scr[pl.ds(at, CHUNK), :].astype(jnp.bfloat16)
                waiting = []

                def collect():
                    cols, factor, probs = waiting.pop(0)
                    acc_scr[:, cols] = acc_scr[:, cols] * factor + lax.dot_general(
                        vals,
                        probs,
                        (((0,), (0,)), ((), ())),
                        preferred_element_type=jnp.float32,
                    )

                ahead = [s_scr[r * ROWS : (r + 1) * ROWS, :] for r in range(GROUPS)]
                for part in range(parts):
                    cols = slice(part * LANES, (part + 1) * LANES)
                    now, ahead = ahead, []
                    if masked:
                        for r in range(GROUPS):
                            key_pos = kpos_scr[pl.ds(at + r * ROWS, ROWS), :]
                            key_pos = jnp.concatenate([key_pos] * (LANES // HD), axis=1)
                            allowed = (key_pos <= qpos_ref[pl.ds(tile, 1), cols]) & (
                                key_pos >= qstart_ref[pl.ds(tile, 1), cols]
                            )
                            now[r] = jnp.where(allowed, now[r], LOW)
                    high = now[0]
                    for scores in now[1:]:
                        high = jnp.maximum(high, scores)
                    old = m_scr[:, cols]
                    new = jnp.maximum(old, jnp.max(high, axis=0, keepdims=True))
                    m_scr[:, cols] = new
                    factor = jnp.exp2((old - new) * SCALE)
                    probs, total = [], None
                    for r, scores in enumerate(now):
                        if part + 1 < parts:
                            ahead.append(score(tile, at, part + 1, r))
                        else:
                            ahead.append(score(tile, after, 0, r))
                        prob = jnp.exp2((scores - new) * SCALE)
                        total = prob if total is None else total + prob
                        probs.append(prob.astype(jnp.bfloat16))
                    l_scr[:, cols] = l_scr[:, cols] * factor + jnp.sum(
                        total, axis=0, keepdims=True
                    )
                    waiting.append((cols, factor, jnp.concatenate(probs, axis=0)))
                    if part:
                        collect()
                collect()
                for r in range(GROUPS):
                    s_scr[r * ROWS : (r + 1) * ROWS, :] = ahead[r]

            pl.when(edge)(lambda: block(True))
            pl.when(jnp.logical_not(edge))(lambda: block(False))
            return carry

        lax.fori_loop(0, steps, one_step, 0)
        total = jnp.where(l_scr[...] > 0, l_scr[...], 1.0)
        part = (acc_scr[...] / total).T.astype(jnp.bfloat16)
        lse = m_scr[...] * SCALE + jnp.log2(total)
        high = lse.astype(jnp.bfloat16).astype(jnp.float32)
        mid = (lse - high).astype(jnp.bfloat16).astype(jnp.float32)
        stats = (high, mid, lse - high - mid)
        xl4 = ((tile >> 1) ^ lax.axis_index("xl")) * 4
        half = tile & 1
        rows = pl.multiple_of(half * HALF, 16)
        for d in range(4):
            out_ref[xl4 + d, pl.ds(rows, HALF), :] = part[d * HALF : (d + 1) * HALF]
            for n, stat in enumerate(stats):
                if d % 2:
                    stat = pltpu.roll(
                        jnp.broadcast_to(stat, (8, TILE)), TILE - 64, 1
                    )[:1]
                base = d * HALF - (d % 2) * 64
                for w in range(2):
                    st_scr[xl4 + d, pl.ds(half * 6 + n * 2 + w, 1), :] = stat[
                        :, base + w * 128 : base + (w + 1) * 128
                    ]
        return carry

    lax.fori_loop(0, 4, one_tile, 0)
    for dest in range(TEAM_SIZE):
        out_ref[dest, TOK:, :] = st_scr[dest].astype(jnp.bfloat16)


def project_kernel(got_ref, w0_ref, w1_ref, out_ref, att_scr):
    for half in range(2):
        sides = []
        for w in range(2):
            lse = []
            for k in range(TEAM_SIZE):
                stat = got_ref[k, TOK:, :].astype(jnp.float32)
                row = half * 6 + w
                lse.append(
                    stat[row : row + 1] + stat[row + 2 : row + 3] + stat[row + 4 : row + 5]
                )
            lse = jnp.concatenate(lse, axis=0)
            weight = jnp.exp2(lse - jnp.max(lse, axis=0, keepdims=True))
            weight = weight / jnp.sum(weight, axis=0, keepdims=True)
            sides.append(weight.T)
        weight = jnp.concatenate([sides[0], sides[1][:64]], axis=0)
        total = jnp.zeros((HALF, HD), jnp.float32)
        for k in range(TEAM_SIZE):
            total += weight[:, k : k + 1] * got_ref[
                k, half * HALF : (half + 1) * HALF, :
            ].astype(jnp.float32)
        att_scr[half] = total.astype(jnp.bfloat16)
    own = lax.axis_index("zl") * 2 + lax.axis_index("core")
    out = None
    for w_ref, part, flip in ((w0_ref, 0, 0), (w0_ref, 1, 2), (w1_ref, 0, 1), (w1_ref, 1, 3)):
        rows = pl.multiple_of((own ^ flip) * QUART, 16)
        att = jnp.concatenate(
            [att_scr[half, pl.ds(rows, QUART), :] for half in range(2)], axis=0
        )
        term = jnp.dot(att, w_ref[part], preferred_element_type=jnp.float32)
        out = term if out is None else out + term
    out_ref[...] = out.astype(jnp.bfloat16)


def per_device(queries, keys, values, block_of_slot, doc_lengths, out_weight):
    hbm = pl.BlockSpec(memory_space=pltpu.HBM)
    smem = pl.BlockSpec(memory_space=pltpu.SMEM)
    vmem = pl.BlockSpec(memory_space=pltpu.VMEM)
    spread = pl.pallas_call(
        spread_kernel,
        out_shape=jax.ShapeDtypeStruct((SRC, 4 * KROWS, HD), jnp.bfloat16),
        in_specs=[hbm, hbm],
        out_specs=hbm,
        scratch_shapes=[
            pltpu.VMEM((2, 4 * KROWS, HD), jnp.bfloat16),
            pltpu.SemaphoreType.DMA((8,)),
            pltpu.SemaphoreType.DMA((SRC,)),
        ],
        name="spread",
    )(keys, values)
    spread, queries, out_weight = lax.optimization_barrier(
        (spread, queries, out_weight)
    )
    kv = lax.all_to_all(spread, DP, 0, 0, tiled=True)
    flip = [(0, 1), (1, 0)]
    q_side = lax.ppermute(queries, "xl", flip)
    q = lax.all_gather(queries, ("zl", "core"), axis=0, tiled=True)
    q_side = lax.all_gather(q_side, ("zl", "core"), axis=0, tiled=True)
    w_side = lax.ppermute(out_weight, "zl", flip)

    lane = np.arange(TILE)
    in_half = lane % QUART // 16 * 64 + lane // HALF * 16 + lane % 16
    i32 = jnp.int32
    tiles, q_pos, q_start = pl.pallas_call(
        table_kernel,
        out_shape=(
            jax.ShapeDtypeStruct((4, 4), i32),
            jax.ShapeDtypeStruct((4, TILE), i32),
            jax.ShapeDtypeStruct((4, TILE), i32),
        ),
        in_specs=[smem, smem, vmem],
        out_specs=(smem, vmem, vmem),
        compiler_params=pltpu.CompilerParams(vmem_limit_bytes=8 << 20),
        name="tables",
    )(block_of_slot, doc_lengths, jnp.asarray(in_half[None, :], i32))

    attend = pl.pallas_call(
        attend_kernel,
        out_shape=jax.ShapeDtypeStruct((TEAM_SIZE, SEND, HD), jnp.bfloat16),
        in_specs=[smem, smem, vmem, vmem, vmem, vmem, vmem],
        out_specs=vmem,
        scratch_shapes=[
            pltpu.VMEM((PAD, HD), jnp.int32),
            pltpu.VMEM((PAD, HD), jnp.float32),
            pltpu.VMEM((PAD, HD), jnp.float32),
            pltpu.VMEM((4, TILE, HD), jnp.bfloat16),
            pltpu.VMEM((CHUNK, LANES), jnp.float32),
            pltpu.VMEM((1, TILE), jnp.float32),
            pltpu.VMEM((1, TILE), jnp.float32),
            pltpu.VMEM((HD, TILE), jnp.float32),
            pltpu.VMEM((TEAM_SIZE, STAT, HD), jnp.float32),
        ],
        compiler_params=pltpu.CompilerParams(vmem_limit_bytes=16 << 20),
        cost_estimate=pl.CostEstimate(
            flops=4 * 4 * TILE * KEYS * HD,
            transcendentals=4 * TILE * KEYS,
            bytes_accessed=4 << 20,
        ),
        name="attend",
    )
    sent = attend(block_of_slot, tiles, kv, q, q_side, q_pos, q_start)
    _, w_side = lax.optimization_barrier((sent, w_side))
    got = lax.all_to_all(sent, TEAM, 0, 0, tiled=True)
    w0 = jnp.stack([out_weight, w_side])
    w1 = lax.ppermute(w0, "core", flip)
    terms = pl.pallas_call(
        project_kernel,
        out_shape=jax.ShapeDtypeStruct((TOK // 4, out_weight.shape[1]), jnp.bfloat16),
        in_specs=[vmem, vmem, vmem],
        out_specs=vmem,
        scratch_shapes=[pltpu.VMEM((2, HALF, HD), jnp.bfloat16)],
        compiler_params=pltpu.CompilerParams(vmem_limit_bytes=16 << 20),
        name="project",
    )(got, w0, w1)
    parts = lax.all_to_all(
        terms.reshape(6, 16, -1), Z6, 0, 0, tiled=True
    )
    return jnp.sum(parts.astype(jnp.float32), axis=0).astype(jnp.bfloat16)


def solution(mesh):
    fine = Mesh(mesh.devices.reshape(SIZES), AXES)
    return jax.shard_map(
        per_device,
        mesh=fine,
        in_specs=(P(DP, HEAD), P(DP, None), P(DP, None), P(), P(), P(HEAD, None)),
        out_specs=P(DP + HEAD, None),
        check_vma=False,
    )
```

```python
import math

import jax
import jax.numpy as jnp
import numpy as np
from jax import lax
from jax.experimental import pallas as pl
from jax.experimental.pallas import tpu as pltpu
from jax.sharding import Mesh, PartitionSpec as P

AXES = ("y", "xh", "xl", "zh", "zm", "zl", "core")
SIZES = (8, 2, 2, 3, 2, 2, 2)
DP = ("y", "xh", "xl")
HEAD = ("zh", "zm", "zl", "core")
TEAM = ("xl", "zl", "core")
Z6 = ("zh", "zm")

TOK = 384
HALF = 192
HD = 128
QUART = 48
KROWS = 24
SRC = 32
PIECES = 2 * SRC
CHUNK = 256
KEYS = PIECES * KROWS
PAD = KEYS + CHUNK
TILE = 4 * HALF
LANES = 256
ROWS = 128
GROUPS = CHUNK // ROWS
TEAM_SIZE = 8
STAT = 16
SEND = TOK + STAT
LOW = -1e30
FAR = 1 << 20
SCALE = math.log2(math.e) / math.sqrt(HD)


def team_index():
    own = lax.axis_index("zl") * 2 + lax.axis_index("core")
    return lax.axis_index("xl") * 4 + own


def start_of(pos, bounds):
    start = jnp.zeros_like(pos)
    for bound in bounds:
        start = jnp.where(pos >= bound, jnp.maximum(start, bound), start)
    return start


def spread_kernel(
    slot_ref,
    len_ref,
    lane_ref,
    k_hbm,
    v_hbm,
    out_hbm,
    tile_ref,
    qpos_ref,
    qstart_ref,
    buf,
    in_sem,
    out_sem,
):
    own = lax.axis_index("zl") * 2 + lax.axis_index("core")
    col = pl.multiple_of(lax.axis_index("zh") * HD, HD)
    loads = []
    for side in range(2):
        row = pl.multiple_of((side * 4 + own) * KROWS, 8)
        for n, src in enumerate((k_hbm, v_hbm)):
            for half in range(2):
                loads.append(
                    pltpu.make_async_copy(
                        src.at[pl.ds(half * HALF + row, KROWS), pl.ds(col, HD)],
                        buf.at[side, pl.ds((2 * n + half) * KROWS, KROWS), :],
                        in_sem.at[4 * side + 2 * n + half],
                    )
                )
    for copy in loads:
        copy.start()
    for copy in loads:
        copy.wait()
    stores = [
        pltpu.make_async_copy(buf.at[n % 2], out_hbm.at[n], out_sem.at[n]) for n in range(SRC)
    ]
    for copy in stores:
        copy.start()
    here = lax.axis_index("y") * 2 + lax.axis_index("xh")
    bounds = [len_ref[0]]
    for n in range(1, len_ref.shape[0] - 1):
        bounds.append(bounds[-1] + len_ref[n])
    for tile in range(4):
        rel, half = divmod(tile, 2)
        block = slot_ref[4 * here + 2 * (lax.axis_index("xl") ^ rel) + half]
        base = block * HALF
        low = lax.div(start_of(base, bounds), HALF)
        tile_ref[tile, 0] = low
        tile_ref[tile, 1] = lax.div((block + 1 - low) * KROWS + CHUNK - 1, CHUNK)
        tile_ref[tile, 2] = base
        tile_ref[tile, 3] = start_of(base + HALF - 1, bounds)
        pos = lane_ref[...] + base
        qpos_ref[tile : tile + 1, :] = pos
        qstart_ref[tile : tile + 1, :] = start_of(pos, bounds)
    for copy in stores:
        copy.wait()


def attend_kernel(
    slot_ref,
    tile_ref,
    kv_ref,
    q_own_ref,
    q_side_ref,
    qpos_ref,
    qstart_ref,
    out_ref,
    kpos_scr,
    k_scr,
    v_scr,
    q_scr,
    s_scr,
    m_scr,
    l_scr,
    acc_scr,
    st_scr,
):
    for piece in range(PIECES):
        src, half = divmod(piece, 2)
        at = pl.multiple_of(slot_ref[piece] * KROWS, 8)
        for n, scr in enumerate((k_scr, v_scr)):
            rows = slice((2 * n + half) * KROWS, (2 * n + half + 1) * KROWS)
            scr[pl.ds(at, KROWS), :] = kv_ref[src, rows, :].astype(jnp.float32)
    k_scr[KEYS:, :] = jnp.zeros((CHUNK, HD), jnp.float32)
    v_scr[KEYS:, :] = jnp.zeros((CHUNK, HD), jnp.float32)
    st_scr[...] = jnp.zeros_like(st_scr)
    row = lax.broadcasted_iota(jnp.int32, (KROWS, HD), 0) + team_index() * KROWS
    for n in range(PIECES):
        kpos_scr[n * KROWS : (n + 1) * KROWS, :] = row + n * HALF
    kpos_scr[KEYS:, :] = jnp.full((PAD - KEYS, HD), FAR, jnp.int32)

    for tile in range(4):
        q_ref = (q_own_ref, q_side_ref)[tile // 2]
        half = tile % 2
        for d in range(4):
            for j in range(4):
                for z3 in range(3):
                    to = d * HALF + j * QUART + z3 * 16
                    of = j * TOK + half * HALF + z3 * 64 + d * 16
                    q_scr[tile, to : to + 16, :] = q_ref[of : of + 16, :]

    def score(tile, at, part, r):
        return lax.dot_general(
            k_scr[pl.ds(at + r * ROWS, ROWS), :].astype(jnp.bfloat16),
            q_scr[tile, part * LANES : (part + 1) * LANES, :],
            (((1,), (1,)), ((), ())),
            preferred_element_type=jnp.float32,
        )

    def one_tile(tile, carry):
        low, steps, q_first, start_last = (tile_ref[tile, n] for n in range(4))
        m_scr[...] = jnp.full_like(m_scr, LOW)
        l_scr[...] = jnp.zeros_like(l_scr)
        acc_scr[...] = jnp.zeros_like(acc_scr)

        start = pl.multiple_of(low * KROWS, 8)
        for r in range(GROUPS):
            s_scr[r * ROWS : (r + 1) * ROWS, :] = score(tile, start, 0, r)

        def one_step(step, carry):
            first = low * KROWS + step * CHUNK
            at = pl.multiple_of(first, 8)
            first_pos = lax.div(first, KROWS) * HALF
            last_pos = lax.div(first + CHUNK - 1, KROWS) * HALF + HALF - 1
            edge = (last_pos > q_first) | (first_pos < start_last)

            after = pl.multiple_of(jnp.minimum(first + CHUNK, KEYS), 8)

            def block(masked):
                parts = TILE // LANES
                vals = v_scr[pl.ds(at, CHUNK), :].astype(jnp.bfloat16)
                waiting = []

                def collect():
                    cols, factor, probs = waiting.pop(0)
                    acc_scr[:, cols] = acc_scr[:, cols] * factor + lax.dot_general(
                        vals,
                        probs,
                        (((0,), (0,)), ((), ())),
                        preferred_element_type=jnp.float32,
                    )

                ahead = [s_scr[r * ROWS : (r + 1) * ROWS, :] for r in range(GROUPS)]
                for part in range(parts):
                    cols = slice(part * LANES, (part + 1) * LANES)
                    now, ahead = ahead, []
                    if masked:
                        for r in range(GROUPS):
                            key_pos = kpos_scr[pl.ds(at + r * ROWS, ROWS), :]
                            key_pos = jnp.concatenate([key_pos] * (LANES // HD), axis=1)
                            allowed = (key_pos <= qpos_ref[pl.ds(tile, 1), cols]) & (
                                key_pos >= qstart_ref[pl.ds(tile, 1), cols]
                            )
                            now[r] = jnp.where(allowed, now[r], LOW)
                    high = now[0]
                    for scores in now[1:]:
                        high = jnp.maximum(high, scores)
                    old = m_scr[:, cols]
                    new = jnp.maximum(old, jnp.max(high, axis=0, keepdims=True))
                    m_scr[:, cols] = new
                    factor = jnp.exp2((old - new) * SCALE)
                    probs, total = [], None
                    for r, scores in enumerate(now):
                        if part + 1 < parts:
                            ahead.append(score(tile, at, part + 1, r))
                        else:
                            ahead.append(score(tile, after, 0, r))
                        prob = jnp.exp2((scores - new) * SCALE)
                        total = prob if total is None else total + prob
                        probs.append(prob.astype(jnp.bfloat16))
                    l_scr[:, cols] = l_scr[:, cols] * factor + jnp.sum(
                        total, axis=0, keepdims=True
                    )
                    waiting.append((cols, factor, jnp.concatenate(probs, axis=0)))
                    if part:
                        collect()
                collect()
                for r in range(GROUPS):
                    s_scr[r * ROWS : (r + 1) * ROWS, :] = ahead[r]

            pl.when(edge)(lambda: block(True))
            pl.when(jnp.logical_not(edge))(lambda: block(False))
            return carry

        lax.fori_loop(0, steps, one_step, 0)
        total = jnp.where(l_scr[...] > 0, l_scr[...], 1.0)
        part = (acc_scr[...] / total).T.astype(jnp.bfloat16)
        lse = m_scr[...] * SCALE + jnp.log2(total)
        high = lse.astype(jnp.bfloat16).astype(jnp.float32)
        mid = (lse - high).astype(jnp.bfloat16).astype(jnp.float32)
        stats = (high, mid, lse - high - mid)
        xl4 = ((tile >> 1) ^ lax.axis_index("xl")) * 4
        half = tile & 1
        rows = pl.multiple_of(half * HALF, 16)
        for d in range(4):
            out_ref[xl4 + d, pl.ds(rows, HALF), :] = part[d * HALF : (d + 1) * HALF]
            for n, stat in enumerate(stats):
                if d % 2:
                    stat = pltpu.roll(
                        jnp.broadcast_to(stat, (8, TILE)), TILE - 64, 1
                    )[:1]
                base = d * HALF - (d % 2) * 64
                for w in range(2):
                    st_scr[xl4 + d, pl.ds(half * 6 + n * 2 + w, 1), :] = stat[
                        :, base + w * 128 : base + (w + 1) * 128
                    ]
        return carry

    lax.fori_loop(0, 4, one_tile, 0)
    for dest in range(TEAM_SIZE):
        out_ref[dest, TOK:, :] = st_scr[dest].astype(jnp.bfloat16)


def project_kernel(got_ref, w0_ref, w1_ref, out_ref, att_scr):
    for half in range(2):
        sides = []
        for w in range(2):
            lse = []
            for k in range(TEAM_SIZE):
                stat = got_ref[k, TOK:, :].astype(jnp.float32)
                row = half * 6 + w
                lse.append(
                    stat[row : row + 1] + stat[row + 2 : row + 3] + stat[row + 4 : row + 5]
                )
            lse = jnp.concatenate(lse, axis=0)
            weight = jnp.exp2(lse - jnp.max(lse, axis=0, keepdims=True))
            weight = weight / jnp.sum(weight, axis=0, keepdims=True)
            sides.append(weight.T)
        weight = jnp.concatenate([sides[0], sides[1][:64]], axis=0)
        total = jnp.zeros((HALF, HD), jnp.float32)
        for k in range(TEAM_SIZE):
            total += weight[:, k : k + 1] * got_ref[
                k, half * HALF : (half + 1) * HALF, :
            ].astype(jnp.float32)
        att_scr[half] = total.astype(jnp.bfloat16)
    own = lax.axis_index("zl") * 2 + lax.axis_index("core")
    out = None
    for w_ref, part, flip in ((w0_ref, 0, 0), (w0_ref, 1, 2), (w1_ref, 0, 1), (w1_ref, 1, 3)):
        rows = pl.multiple_of((own ^ flip) * QUART, 16)
        att = jnp.concatenate(
            [att_scr[half, pl.ds(rows, QUART), :] for half in range(2)], axis=0
        )
        term = jnp.dot(att, w_ref[part], preferred_element_type=jnp.float32)
        out = term if out is None else out + term
    out_ref[...] = out.astype(jnp.bfloat16)


def per_device(queries, keys, values, block_of_slot, doc_lengths, out_weight):
    hbm = pl.BlockSpec(memory_space=pltpu.HBM)
    smem = pl.BlockSpec(memory_space=pltpu.SMEM)
    vmem = pl.BlockSpec(memory_space=pltpu.VMEM)
    lane = np.arange(TILE)
    in_half = lane % QUART // 16 * 64 + lane // HALF * 16 + lane % 16
    i32 = jnp.int32
    spread, tiles, q_pos, q_start = pl.pallas_call(
        spread_kernel,
        out_shape=(
            jax.ShapeDtypeStruct((SRC, 4 * KROWS, HD), jnp.bfloat16),
            jax.ShapeDtypeStruct((4, 4), i32),
            jax.ShapeDtypeStruct((4, TILE), i32),
            jax.ShapeDtypeStruct((4, TILE), i32),
        ),
        in_specs=[smem, smem, vmem, hbm, hbm],
        out_specs=(hbm, smem, vmem, vmem),
        scratch_shapes=[
            pltpu.VMEM((2, 4 * KROWS, HD), jnp.bfloat16),
            pltpu.SemaphoreType.DMA((8,)),
            pltpu.SemaphoreType.DMA((SRC,)),
        ],
        name="spread",
    )(
        block_of_slot,
        doc_lengths,
        jnp.asarray(in_half[None, :], i32),
        keys,
        values,
    )
    spread, queries, out_weight = lax.optimization_barrier(
        (spread, queries, out_weight)
    )
    kv = lax.all_to_all(spread, DP, 0, 0, tiled=True)
    flip = [(0, 1), (1, 0)]
    q_side = lax.ppermute(queries, "xl", flip)
    q = lax.all_gather(queries, ("zl", "core"), axis=0, tiled=True)
    q_side = lax.all_gather(q_side, ("zl", "core"), axis=0, tiled=True)
    w_side = lax.ppermute(out_weight, "zl", flip)

    attend = pl.pallas_call(
        attend_kernel,
        out_shape=jax.ShapeDtypeStruct((TEAM_SIZE, SEND, HD), jnp.bfloat16),
        in_specs=[smem, smem, vmem, vmem, vmem, vmem, vmem],
        out_specs=vmem,
        scratch_shapes=[
            pltpu.VMEM((PAD, HD), jnp.int32),
            pltpu.VMEM((PAD, HD), jnp.float32),
            pltpu.VMEM((PAD, HD), jnp.float32),
            pltpu.VMEM((4, TILE, HD), jnp.bfloat16),
            pltpu.VMEM((CHUNK, LANES), jnp.float32),
            pltpu.VMEM((1, TILE), jnp.float32),
            pltpu.VMEM((1, TILE), jnp.float32),
            pltpu.VMEM((HD, TILE), jnp.float32),
            pltpu.VMEM((TEAM_SIZE, STAT, HD), jnp.float32),
        ],
        compiler_params=pltpu.CompilerParams(vmem_limit_bytes=16 << 20),
        cost_estimate=pl.CostEstimate(
            flops=4 * 4 * TILE * KEYS * HD,
            transcendentals=4 * TILE * KEYS,
            bytes_accessed=4 << 20,
        ),
        name="attend",
    )
    sent = attend(block_of_slot, tiles, kv, q, q_side, q_pos, q_start)
    _, w_side = lax.optimization_barrier((sent, w_side))
    got = lax.all_to_all(sent, TEAM, 0, 0, tiled=True)
    w0 = jnp.stack([out_weight, w_side])
    w1 = lax.ppermute(w0, "core", flip)
    terms = pl.pallas_call(
        project_kernel,
        out_shape=jax.ShapeDtypeStruct((TOK // 4, out_weight.shape[1]), jnp.bfloat16),
        in_specs=[vmem, vmem, vmem],
        out_specs=vmem,
        scratch_shapes=[pltpu.VMEM((2, HALF, HD), jnp.bfloat16)],
        compiler_params=pltpu.CompilerParams(vmem_limit_bytes=16 << 20),
        name="project",
    )(got, w0, w1)
    parts = lax.all_to_all(
        terms.reshape(6, 16, -1), Z6, 0, 0, tiled=True
    )
    return jnp.sum(parts.astype(jnp.float32), axis=0).astype(jnp.bfloat16)


def solution(mesh):
    fine = Mesh(mesh.devices.reshape(SIZES), AXES)
    return jax.shard_map(
        per_device,
        mesh=fine,
        in_specs=(P(DP, HEAD), P(DP, None), P(DP, None), P(), P(), P(HEAD, None)),
        out_specs=P(DP + HEAD, None),
        check_vma=False,
    )
```
